128 devices in a mesh: seq: 64 (over x, z, y), head: 2 (over core).
Axes of the slice: x: 4, y: 4, z: 4, core: 2. Of those that a mesh axis runs over, the one named last changes fastest.
Arguments:
- hidden: bfloat16 [16384, 2048], P('seq', 'head'), may hold values from -16 to 16
- proj_weights: bfloat16 [2048, 3, 1024], P(None, None, 'head'), may hold values from -0.125 to 0.125
- level_mix: float32 [15, 8, 16384], P(None, 'head', 'seq'), may hold values from 0.25 to 1
- out_grad: bfloat16 [16384, 1024], P('seq', 'head'), may hold values from -1.5 to 1.5
Outputs:
- attended: bfloat16 [16384, 1024], P('seq', 'head')
- input_grad: bfloat16 [16384, 2048], P('seq', 'head')
- weight_grad: float32 [2048, 3, 1024], P('seq', None, 'head')
- level_grad: float32 [15, 8, 16384], P(None, 'head', 'seq')
The draws below stay inside these ranges and needn't reach their ends.
All inputs are finite; a program needn't handle non-finite values.
Results may differ from the reference program's by a relative error of at most 0.0062.
Values may be sent and summed in bfloat16 or wider, within the bound.
No kernel may reach another device: no remote copies, remote signals or barrier semaphores. Data moves between devices by JAX's collectives and lax.ppermute only.
A program may use at most 128 MiB of HBM per device.

```python
import math
import jax
import jax.numpy as jnp
from jax import lax

D = 2048
HEADS = 8
DH = 128
TOKENS_PER_BLOCK = 256
HD = 1024
TOKENS = 16384
LOG_TOK = 8
LOG_SEQ = 6
LEVELS = 15
N_SEQ = 64


def with_spikes(entries, rng, source, target, blocks, factor):
    owner, partner = [(jnp.arange(entries.shape[dim]) // (entries.shape[dim] // blocks)).reshape([-1 if axis == dim else 1 for axis in range(entries.ndim)]) for dim in (source, target)]
    chosen = jax.random.permutation(rng, blocks)[partner]
    strong = (owner == chosen) | (owner == (partner + blocks // 2) % blocks)
    return jnp.where(strong, factor * entries, entries)


def block_scale(stream_key, shape, split, least, top_value):
    loudness, own = 1.0, jax.random.fold_in(stream_key, 6)
    for axis_at, blocks in split:
        heights = jnp.exp(jax.random.uniform(jax.random.fold_in(own, axis_at), (blocks,), jnp.float32, least / len(split), top_value / len(split)))
        loudness = loudness * jnp.repeat(heights, shape[axis_at] // blocks).reshape([-1 if axis == axis_at else 1 for axis in range(len(shape))])
    return loudness


def noise(key, shape, scale, reach, shards=(), kind=jnp.bfloat16):
    values = jax.random.normal(key, shape, jnp.float32) * scale
    if len(shards) > 0:
        values = block_scale(key, shape, shards, -0.22, 0.18) * values
    return jnp.clip(values, min=-reach, max=reach).astype(kind)


def bell_draw_with(stream_key, extent, scale, limit, split, heavy, kind=jnp.bfloat16):
    values = scale * jax.random.normal(stream_key, extent, jnp.float32)
    if split:
        values = values * block_scale(stream_key, extent, split, -0.22, 0.18)
    return jnp.clip(with_spikes(values, jax.random.fold_in(stream_key, 3), *heavy), -limit, limit).astype(kind)


def setup_inputs(seed: int = 0) -> dict:
    key_of = jax.random.split(jax.random.key(seed), 5)
    return {
        "hidden": bell_draw_with(key_of[0], (TOKENS, D), 1.0, 16.0, ((0, 64), (1, 2)), (0, 1, 64, 4.0)),
        "proj_weights": noise(key_of[1], (D, 3, HD), D ** -0.5, 0.125, ((2, 2),)),
        "level_mix": jnp.clip(jnp.exp(math.log(1.0) - 1.3862944 * jax.random.uniform(key_of[2], (LEVELS, HEADS, TOKENS), jnp.float32) ** block_scale(key_of[2], (LEVELS, HEADS, TOKENS), ((1, 2), (2, 64)), -0.2, 0.2)), 0.25, 1.0),
        "out_grad": noise(key_of[3], (TOKENS, HD), 0.25, 1.5, ((0, 64), (1, 2))),
    }


UPPER_LIMIT = lax.Precision.HIGHEST


def digit_count(numbers, digits):
    counted = jnp.zeros(numbers.shape, jnp.int32)
    for place in range(digits):
        counted = counted + (numbers >= (1 << place)).astype(jnp.int32)
    return counted


def level_table(count, digits):
    positions = jnp.arange(count, dtype=jnp.int32)
    levels = digit_count(jnp.bitwise_xor(positions[:, None], positions[None, :]), digits)
    return jnp.where(positions[None, :] <= positions[:, None], levels, -1)


def level_scale(count):
    order = jnp.arange(count, dtype=jnp.float32)
    return jnp.where(order < 0.5, 1.0, jnp.exp2(-0.5 * (order - 1.0)))


def inner_head(queries, key_rows, values, grads, weights, table):
    scores = jnp.dot(queries, key_rows.T, preferred_element_type=jnp.float32)
    weighting = jnp.zeros(scores.shape, jnp.float32)
    for level_no in range(weights.shape[0]):
        weighting = jnp.where(table == level_no, weights[level_no][:, None], weighting)
    mixed = (weighting * scores).astype(jnp.bfloat16)
    result = jnp.dot(mixed, values, preferred_element_type=jnp.float32)
    mix_grad = jnp.dot(grads, values.T, preferred_element_type=jnp.float32)
    value_grad = jnp.dot(mixed.T, grads, preferred_element_type=jnp.float32)
    score_grad = (weighting * mix_grad).astype(jnp.bfloat16)
    query_gradient = jnp.dot(score_grad, key_rows, preferred_element_type=jnp.float32)
    key_grad = jnp.dot(score_grad.T, queries, preferred_element_type=jnp.float32)
    product = mix_grad * scores
    level_grad = jnp.stack([jnp.sum(jnp.where(table == level_no, product, 0.0), axis=1) for level_no in range(weights.shape[0])])
    return result, query_gradient, key_grad, value_grad, level_grad


def reference(hidden, proj_weights, level_mix, out_grad):
    root = DH ** -0.5
    inner_levels = LOG_TOK + 1
    projected = [jnp.dot(hidden, proj_weights[:, part_no, :], preferred_element_type=jnp.float32) for part_no in range(3)]
    queries = (projected[0] * root).astype(jnp.bfloat16)
    key_rows = projected[1].astype(jnp.bfloat16)
    values = projected[2].astype(jnp.bfloat16)

    def by_block(array):
        return array.reshape(N_SEQ, TOKENS_PER_BLOCK, HEADS, DH).transpose(0, 2, 1, 3)

    block_queries = by_block(queries)
    block_keys = by_block(key_rows)
    block_values = by_block(values)
    block_grads = by_block(out_grad)
    scale = level_scale(LEVELS)
    level_weights = (level_mix * scale[:, None, None]).reshape(LEVELS, HEADS, N_SEQ, TOKENS_PER_BLOCK).transpose(2, 0, 1, 3)
    states = jnp.einsum("chtk,chtv->chkv", block_keys.astype(jnp.float32), block_values.astype(jnp.float32), precision=UPPER_LIMIT)
    stretch = jnp.arange(N_SEQ, dtype=jnp.int32)
    apart = digit_count(jnp.bitwise_xor(stretch[:, None], stretch[None, :]), LOG_SEQ)
    earlier = stretch[None, :] < stretch[:, None]
    member = jnp.stack([jnp.where(earlier & (apart == bit_no + 1), 1.0, 0.0) for bit_no in range(LOG_SEQ)], axis=1).astype(jnp.float32)
    buckets = jnp.einsum("cjd,dhkv->cjhkv", member, states, precision=UPPER_LIMIT)
    table = level_table(TOKENS_PER_BLOCK, LOG_TOK)

    def one_block(bundle):
        head_queries, key_per_head, value_per_head, head_grads, weights, bucket = bundle
        inner_weights = weights[:inner_levels].transpose(1, 0, 2)
        inner = lax.map(lambda pack: inner_head(pack[0], pack[1], pack[2], pack[3], pack[4], table), (head_queries, key_per_head, value_per_head, head_grads, inner_weights))
        inner_out, inner_query, inner_key, inner_value, inner_level = inner
        outer_weights = weights[inner_levels:]
        query_wide = head_queries.astype(jnp.float32)
        grads_wide = head_grads.astype(jnp.float32)
        reads = jnp.einsum("htk,jhkv->jhtv", query_wide, bucket, precision=UPPER_LIMIT)
        outer_out = jnp.sum(outer_weights[..., None] * reads, axis=0)
        outer_level = jnp.sum(grads_wide[None] * reads, axis=-1)
        weighted = outer_weights[..., None] * grads_wide[None]
        outer_query = jnp.einsum("jhtv,jhkv->htk", weighted, bucket, precision=UPPER_LIMIT)
        bucket_grad = jnp.einsum("htk,jhtv->jhkv", query_wide, weighted, precision=UPPER_LIMIT)
        attended = (inner_out + outer_out).astype(jnp.bfloat16)
        grad_queries = ((inner_query + outer_query) * root).astype(jnp.bfloat16)
        level_grad = jnp.concatenate([inner_level.transpose(1, 0, 2), outer_level], axis=0)
        return attended, grad_queries, inner_key, inner_value, level_grad, bucket_grad

    results = lax.map(one_block, (block_queries, block_keys, block_values, block_grads, level_weights, buckets))
    attended_blocks, query_blocks, inner_keys, inner_values, level_blocks, bucket_grads = results
    state_grads = jnp.einsum("cjd,cjhkv->dhkv", member, bucket_grads, precision=UPPER_LIMIT)
    outer_key = jnp.einsum("chtv,chkv->chtk", block_values.astype(jnp.float32), state_grads, precision=UPPER_LIMIT)
    outer_value = jnp.einsum("chtk,chkv->chtv", block_keys.astype(jnp.float32), state_grads, precision=UPPER_LIMIT)
    key_blocks = (inner_keys + outer_key).astype(jnp.bfloat16)
    value_blocks = (inner_values + outer_value).astype(jnp.bfloat16)

    def by_token(array):
        return array.transpose(0, 2, 1, 3).reshape(TOKENS, HD)

    attended = by_token(attended_blocks)
    gradients = [by_token(query_blocks), by_token(key_blocks), by_token(value_blocks)]
    summed_input = jnp.zeros((TOKENS, D), jnp.float32)
    for part_no in range(3):
        summed_input = summed_input + jnp.dot(gradients[part_no], proj_weights[:, part_no, :].T, preferred_element_type=jnp.float32)
    input_grad = summed_input.astype(jnp.bfloat16)
    weight_grad = jnp.stack([jnp.dot(hidden.T, gradients[part_no], preferred_element_type=jnp.float32) * TOKENS ** -0.5 for part_no in range(3)], axis=1)
    level_grad = level_blocks.transpose(1, 2, 0, 3).reshape(LEVELS, HEADS, TOKENS) * scale[:, None, None]
    return attended, input_grad, weight_grad, level_grad
```

```python
import functools

import jax
import jax.numpy as jnp
from jax import lax
from jax.experimental import pallas as pl
from jax.experimental.pallas import tpu as pltpu
from jax.sharding import Mesh
from jax.sharding import PartitionSpec as P

DH = 128
SEQ = ("seq_0", "seq_1", "seq_2")
ALL = SEQ + ("head",)
BF = jnp.bfloat16
F32 = jnp.float32
X, Z, Y = 0, 1, 2


def scale_of(level):
    return 1.0 if level == 0 else 2.0 ** (-(level - 1) / 2)


def places():
    return [
        (x, z, y, h) for x in range(4) for z in range(4) for y in range(4) for h in range(2)
    ]


def index_of(place):
    x, z, y, h = place
    return ((x * 4 + z) * 4 + y) * 2 + h


def shifted(value, axes, step, which="all"):
    pairs = []
    for place in places():
        axis = axes[place[3]]
        target = list(place)
        target[axis] = (place[axis] + step) % 4
        if which == "up" and target[axis] < place[axis]:
            continue
        if which == "down" and target[axis] > place[axis]:
            continue
        pairs.append((index_of(place), index_of(target)))
    return lax.ppermute(value, ALL, pairs)


def partner(value):
    return lax.ppermute(value, "head", [(0, 1), (1, 0)])


def dot(a, b, dims):
    return lax.dot_general(a, b, (dims, ((), ())), preferred_element_type=F32)


def flag(condition):
    return jnp.where(condition, 1.0, 0.0).astype(F32)


def turned(array):
    return array.astype(F32).T


def state_kernel(pos, q, k, v, g, mix, s_out, b0, b1, b2, b3, b5, u3):
    qt = turned(q[0])
    kt = turned(k[0]).astype(BF)
    gg = g[...]
    s_out[...] = dot(kt, v[0], ((1,), (0,))).astype(BF)

    def grad(j):
        row = mix[0, 9 + j : 10 + j, :] * scale_of(9 + j)
        return dot((qt * row).astype(BF), gg, ((1,), (0,)))

    b0[...] = grad(0).astype(BF)
    b1[...] = grad(1).astype(BF)
    b2[...] = grad(2).astype(BF)
    b3[...] = grad(3).astype(BF)
    g4, g5 = grad(4), grad(5)
    b5[...] = g5.astype(BF)
    two = flag(pos[X] == 2)
    u3[...] = (g5 * two + g4 * (1.0 - two)).astype(BF)


def up_terms(p, low, high):
    one = high * flag(p == 3)
    two = high * flag(p >= 2)
    three = low * flag((p == 1) | (p == 3)) + high * flag(p == 2)
    return one, two, three


def middle_kernel(pos, s, gy1, gy2, gy3, r1, r2, r3, b2, b3, p1, p2, p3, held):
    group = s[...].astype(F32) + gy1[...] + gy2[...] + gy3[...]
    held_now = r1[...].astype(F32) + r2[...] + r3[...]
    held[...] = held_now
    terms = up_terms(pos[Z], b2[...].astype(F32), b3[...].astype(F32))
    group = group.astype(BF)
    for out, term in zip((p1, p2, p3), terms):
        out[:512] = group
        out[512:] = (held_now + term).astype(BF)


def late_kernel(pos, p1, rz1, rz2, rz3, held, b0, b1, group, q1, q2, q3, held_out):
    whole = p1[:512].astype(F32) + rz1[:512] + rz2[:512] + rz3[:512]
    group[...] = whole.astype(BF)
    held_now = held[...] + rz1[512:].astype(F32) + rz2[512:] + rz3[512:]
    held_out[...] = held_now
    terms = up_terms(pos[Y], b0[...].astype(F32), b1[...].astype(F32))
    for out, term in zip((q1, q2, q3), terms):
        out[...] = (held_now + term).astype(BF)


def inner_kernel(q, k, v, g, mix, out_t, query_t, key_out, value_out, level_out, table):
    @pl.when(pl.program_id(0) == 0)
    def _():
        s_at = lax.broadcasted_iota(jnp.int32, (256, 256), 0)
        t_at = lax.broadcasted_iota(jnp.int32, (256, 256), 1)
        apart = s_at ^ t_at
        level = jnp.zeros((256, 256), jnp.int32)
        for place in range(8):
            level = level + (apart >= (1 << place)).astype(jnp.int32)
        table[...] = jnp.where(s_at <= t_at, level, -1)

    qq, kk, vv, gg = q[0], k[0], v[0], g[...]
    kt = turned(kk).astype(BF)
    vt = turned(vv).astype(BF)
    scores = dot(kk, qq, ((1,), (1,)))
    mix_grad = dot(vv, gg, ((1,), (1,)))
    levels = table[...]
    weight = jnp.zeros((256, 256), F32)
    product = scores * mix_grad
    for level in range(9):
        here = levels == level
        weight = jnp.where(here, mix[0, level : level + 1, :] * scale_of(level), weight)
        level_out[0, level : level + 1, :] = jnp.sum(
            jnp.where(here, product, 0.0), axis=0, keepdims=True
        ) * scale_of(level)
    mixed = (weight * scores).astype(BF)
    score_grad = (weight * mix_grad).astype(BF)
    out_t[0] = dot(vt, mixed, ((1,), (0,)))
    query_t[0] = dot(kt, score_grad, ((1,), (0,)))
    key_out[...] = dot(score_grad, qq, ((1,), (0,)))
    value_out[...] = dot(mixed, gg, ((1,), (0,)))


def outer_kernel(
    pos, q, k, v, g, mix, out_t, query_t, key_in, value_in, level_in,
    gy1, gy2, gy3, rz1, rz2, rz3, gx1, gx2, gx3, held, ry1, ry2, ry3,
    attended, grads, level_out,
):
    qt = turned(q[0]).astype(BF)
    gt = turned(g[...])

    def pair(p, one, two, three):
        one, two, three = one[...].astype(F32), two[...].astype(F32), three[...].astype(F32)
        low = one * flag((p == 1) | (p == 3))
        high = one * flag(p == 2) + two * flag(p >= 2) + three * flag(p == 3)
        return low.astype(BF), high.astype(BF)

    buckets = (
        pair(pos[Y], gy1, gy2, gy3) + pair(pos[Z], rz1, rz2, rz3) + pair(pos[X], gx1, gx2, gx3)
    )
    total = out_t[0]
    query = query_t[0]
    level_out[0, :9, :] = level_in[0, :9, :]
    for j, bucket in enumerate(buckets):
        row = mix[0, 9 + j : 10 + j, :] * scale_of(9 + j)
        reads = dot(bucket, qt, ((0,), (0,)))
        total = total + reads * row
        level_out[0, 9 + j : 10 + j, :] = jnp.sum(reads * gt, axis=0, keepdims=True) * scale_of(
            9 + j
        )
        query = query + dot(bucket, (gt * row).astype(BF), ((1,), (0,)))
    attended[...] = total.T.astype(BF)
    grads[0] = (query * DH**-0.5).T.astype(BF)
    state = (held[...] + ry1[...].astype(F32) + ry2[...] + ry3[...]).astype(BF)
    grads[1] = (key_in[...] + dot(v[0], state, ((1,), (1,)))).astype(BF)
    grads[2] = (value_in[...] + dot(k[0], state, ((1,), (0,)))).astype(BF)


def part(index):
    return pl.BlockSpec((1, 256, DH), lambda h: (index, 0, h))


COLUMNS = pl.BlockSpec((256, DH), lambda h: (0, h))
STATE = pl.BlockSpec((DH, DH), lambda h: (h, 0))
MIX = pl.BlockSpec((1, 15, 256), lambda h: (h, 0, 0))
TURNED = pl.BlockSpec((1, DH, 256), lambda h: (h, 0, 0))
SCALARS = pl.BlockSpec(memory_space=pltpu.SMEM)


def shape(dims, kind):
    return jax.ShapeDtypeStruct(dims, kind)


def on_device(hidden, proj_weights, level_mix, out_grad):
    x, z, y = (lax.axis_index(name) for name in SEQ)
    core = lax.axis_index("head")
    first = core == 0
    pos = jnp.stack([x, z, y]).astype(jnp.int32)
    other = partner(hidden)
    features = jnp.concatenate(
        [jnp.where(first, hidden, other), jnp.where(first, other, hidden)], axis=1
    )
    root = jnp.array([DH**-0.5, 1.0, 1.0], F32)[:, None, None]
    projected = (
        jnp.einsum("td,dme->mte", features, proj_weights, preferred_element_type=F32) * root
    ).astype(BF)
    mix = level_mix.transpose(1, 0, 2)

    by_z = features.reshape(256, 4, 4, 128).transpose(0, 2, 1, 3).reshape(256, 2048)
    sorted_features = jnp.where(first, features, by_z)
    line = jnp.where(first, x, z)

    def columns(step):
        return lax.dynamic_slice_in_dim(sorted_features, 512 * ((line + step) % 4), 512, 1)

    hidden_blocks = [columns(0)] + [shifted(columns(n), (X, Z), n) for n in (1, 2, 3)]

    state_shape = shape((512, DH), BF)
    states, b0, b1, b2, b3, b5, u3 = pl.pallas_call(
        state_kernel,
        grid=(4,),
        in_specs=[SCALARS, part(0), part(1), part(2), COLUMNS, MIX],
        out_specs=[STATE] * 7,
        out_shape=[state_shape] * 7,
    )(pos, projected, projected, projected, out_grad, mix)

    def line_of(axis):
        return (axis, axis)

    gy = [shifted(states, line_of(Y), n) for n in (1, 2, 3)]
    rx = [shifted(a, line_of(X), n, "down") for n, a in ((1, b5), (2, b5), (3, u3))]
    out_t, query_t, key_in, value_in, level_in = pl.pallas_call(
        inner_kernel,
        grid=(4,),
        in_specs=[part(0), part(1), part(2), COLUMNS, MIX],
        out_specs=[
            TURNED,
            TURNED,
            COLUMNS,
            COLUMNS,
            pl.BlockSpec((1, 16, 256), lambda h: (h, 0, 0)),
        ],
        out_shape=[
            shape((4, DH, 256), F32),
            shape((4, DH, 256), F32),
            shape((256, 512), F32),
            shape((256, 512), F32),
            shape((4, 16, 256), F32),
        ],
        scratch_shapes=[pltpu.VMEM((256, 256), jnp.int32)],
    )(projected, projected, projected, out_grad, mix)
    whole = pl.BlockSpec(memory_space=pltpu.VMEM)
    p1, p2, p3, held = pl.pallas_call(
        middle_kernel,
        in_specs=[SCALARS] + [whole] * 9,
        out_specs=[whole] * 4,
        out_shape=[shape((1024, DH), BF)] * 3 + [shape((512, DH), F32)],
    )(pos, states, *gy, *rx, b2, b3)
    rz = [shifted(a, line_of(Z), n) for n, a in ((1, p1), (2, p2), (3, p3))]
    group, q1, q2, q3, held = pl.pallas_call(
        late_kernel,
        in_specs=[SCALARS] + [whole] * 7,
        out_specs=[whole] * 5,
        out_shape=[state_shape] * 4 + [shape((512, DH), F32)],
    )(pos, p1, *rz, held, b0, b1)
    ry = [shifted(a, line_of(Y), n) for n, a in ((1, q1), (2, q2), (3, q3))]
    gx = [shifted(group, line_of(X), n, "up") for n in (1, 2, 3)]
    attended, grads, level_grad = pl.pallas_call(
        outer_kernel,
        grid=(4,),
        in_specs=[SCALARS, part(0), part(1), part(2), COLUMNS, MIX, TURNED, TURNED]
        + [COLUMNS, COLUMNS, pl.BlockSpec((1, 16, 256), lambda h: (h, 0, 0))]
        + [STATE] * 13,
        out_specs=[COLUMNS, pl.BlockSpec((3, 256, DH), lambda h: (0, 0, h)), MIX],
        out_shape=[
            shape((256, 512), BF),
            shape((3, 256, 512), BF),
            shape((4, 15, 256), F32),
        ],
    )(
        pos, projected, projected, projected, out_grad, mix, out_t, query_t, key_in, value_in,
        level_in, *gy, *rz, *gx, held, *ry,
    )
    level_grad = level_grad.transpose(1, 0, 2)

    grad_blocks = [grads] + [shifted(grads, (X, Z), n) for n in (1, 2, 3)]

    partial_inputs = jnp.einsum("mte,dme->td", grads, proj_weights, preferred_element_type=F32)
    mine = lax.dynamic_slice_in_dim(partial_inputs, 1024 * core, 1024, 1)
    theirs = lax.dynamic_slice_in_dim(partial_inputs, 1024 * (1 - core), 1024, 1)
    input_grad = (mine + partner(theirs)).astype(BF)

    partial_weights = functools.reduce(
        jnp.add,
        [
            jnp.einsum("td,mte->mde", h, g, preferred_element_type=F32)
            for h, g in zip(hidden_blocks, grad_blocks)
        ],
    )

    def reduced(array, at, axes, rows):
        def rows_of(step):
            return lax.dynamic_slice_in_dim(array, rows * ((at + step) % 4), rows, 1)

        came = [shifted(rows_of(n).astype(BF), axes, n) for n in (1, 2, 3)]
        return rows_of(0) + came[0] + came[1] + came[2]

    partial_weights = reduced(partial_weights, jnp.where(first, z, x), (Z, X), 128)
    partial_weights = reduced(partial_weights, y, (Y, Y), 32)
    weight_grad = (partial_weights * 16384**-0.5).transpose(1, 0, 2)
    return (attended, input_grad, weight_grad, level_grad)


def solution(mesh):
    split = Mesh(mesh.devices.reshape(4, 4, 4, 2), ALL)
    return jax.shard_map(
        on_device,
        mesh=split,
        in_specs=(P(SEQ, "head"), P(None, None, "head"), P(None, "head", SEQ), P(SEQ, "head")),
        out_specs=(P(SEQ, "head"), P(SEQ, "head"), P(SEQ, None, "head"), P(None, "head", SEQ)),
        check_vma=False,
    )
```

```python
import functools

import jax
import jax.numpy as jnp
from jax import lax
from jax.experimental import pallas as pl
from jax.experimental.pallas import tpu as pltpu
from jax.sharding import Mesh
from jax.sharding import PartitionSpec as P


DH = 128
SEQ = ("seq_0", "seq_1", "seq_2")
ALL = SEQ + ("head",)
BF = jnp.bfloat16
F32 = jnp.float32
X, Z, Y = 0, 1, 2


def scale_of(level):
    return 1.0 if level == 0 else 2.0 ** (-(level - 1) / 2)


def places():
    return [
        (x, z, y, h) for x in range(4) for z in range(4) for y in range(4) for h in range(2)
    ]


def index_of(place):
    x, z, y, h = place
    return ((x * 4 + z) * 4 + y) * 2 + h


def shifted(value, axes, step, which="all"):
    pairs = []
    for place in places():
        axis = axes[place[3]]
        target = list(place)
        target[axis] = (place[axis] + step) % 4
        if which == "up" and target[axis] < place[axis]:
            continue
        if which == "down" and target[axis] > place[axis]:
            continue
        pairs.append((index_of(place), index_of(target)))
    return lax.ppermute(value, ALL, pairs)


def partner(value):
    return lax.ppermute(value, "head", [(0, 1), (1, 0)])


def dot(a, b, dims):
    return lax.dot_general(a, b, (dims, ((), ())), preferred_element_type=F32)


def flag(condition):
    return jnp.where(condition, 1.0, 0.0).astype(F32)


def turned(array):
    return array.astype(F32).T


def state_kernel(pos, q, k, v, g, mix, s_out, b0, b1, b2, b3, b5, u3):
    qt = turned(q[0])
    kt = turned(k[0]).astype(BF)
    gg = g[...]
    s_out[...] = dot(kt, v[0], ((1,), (0,))).astype(BF)

    def grad(j):
        row = mix[0, 9 + j : 10 + j, :] * scale_of(9 + j)
        return dot((qt * row).astype(BF), gg, ((1,), (0,)))

    b0[...] = grad(0).astype(BF)
    b1[...] = grad(1).astype(BF)
    b2[...] = grad(2).astype(BF)
    b3[...] = grad(3).astype(BF)
    g4, g5 = grad(4), grad(5)
    b5[...] = g5.astype(BF)
    two = flag(pos[X] == 2)
    u3[...] = (g5 * two + g4 * (1.0 - two)).astype(BF)


def up_terms(p, low, high):
    one = high * flag(p == 3)
    two = high * flag(p >= 2)
    three = low * flag((p == 1) | (p == 3)) + high * flag(p == 2)
    return one, two, three


def middle_kernel(pos, s, gy1, gy2, gy3, r1, r2, r3, b2, b3, p1, p2, p3, held):
    group = s[...].astype(F32) + gy1[...] + gy2[...] + gy3[...]
    held_now = r1[...].astype(F32) + r2[...] + r3[...]
    held[...] = held_now
    terms = up_terms(pos[Z], b2[...].astype(F32), b3[...].astype(F32))
    group = group.astype(BF)
    for out, term in zip((p1, p2, p3), terms):
        out[:512] = group
        out[512:] = (held_now + term).astype(BF)


def late_kernel(pos, p1, rz1, rz2, rz3, held, b0, b1, group, q1, q2, q3, held_out):
    whole = p1[:512].astype(F32) + rz1[:512] + rz2[:512] + rz3[:512]
    group[...] = whole.astype(BF)
    held_now = held[...] + rz1[512:].astype(F32) + rz2[512:] + rz3[512:]
    held_out[...] = held_now
    terms = up_terms(pos[Y], b0[...].astype(F32), b1[...].astype(F32))
    for out, term in zip((q1, q2, q3), terms):
        out[...] = (held_now + term).astype(BF)


def inner_kernel(q, k, v, g, mix, out_t, query_t, key_out, value_out, level_out, table):
    @pl.when(pl.program_id(0) == 0)
    def _():
        s_at = lax.broadcasted_iota(jnp.int32, (256, 256), 0)
        t_at = lax.broadcasted_iota(jnp.int32, (256, 256), 1)
        apart = s_at ^ t_at
        level = jnp.zeros((256, 256), jnp.int32)
        for place in range(8):
            level = level + (apart >= (1 << place)).astype(jnp.int32)
        table[...] = jnp.where(s_at <= t_at, level, -1)

    qq, kk, vv, gg = q[0], k[0], v[0], g[...]
    kt = turned(kk).astype(BF)
    vt = turned(vv).astype(BF)
    scores = dot(kk, qq, ((1,), (1,)))
    mix_grad = dot(vv, gg, ((1,), (1,)))
    levels = table[...]
    weight = jnp.zeros((256, 256), F32)
    product = scores * mix_grad
    for level in range(9):
        here = levels == level
        weight = jnp.where(here, mix[0, level : level + 1, :] * scale_of(level), weight)
        level_out[0, level : level + 1, :] = jnp.sum(
            jnp.where(here, product, 0.0), axis=0, keepdims=True
        ) * scale_of(level)
    mixed = (weight * scores).astype(BF)
    score_grad = (weight * mix_grad).astype(BF)
    out_t[0] = dot(vt, mixed, ((1,), (0,)))
    query_t[0] = dot(kt, score_grad, ((1,), (0,)))
    key_out[...] = dot(score_grad, qq, ((1,), (0,)))
    value_out[...] = dot(mixed, gg, ((1,), (0,)))


def key_value_kernel(k, v, key_in, value_in, held, ry1, ry2, ry3, grads):
    state = (held[...] + ry1[...].astype(F32) + ry2[...] + ry3[...]).astype(BF)
    grads[0] = (key_in[...] + dot(v[0], state, ((1,), (1,)))).astype(BF)
    grads[1] = (value_in[...] + dot(k[0], state, ((1,), (0,)))).astype(BF)


def query_kernel(
    pos, q, g, mix, out_t, query_t, level_in, gy1, gy2, gy3, rz1, rz2, rz3, gx1, gx2, gx3,
    attended, grads, level_out,
):
    qt = turned(q[0]).astype(BF)
    gt = turned(g[...])

    def pair(p, one, two, three):
        one, two, three = one[...].astype(F32), two[...].astype(F32), three[...].astype(F32)
        low = one * flag((p == 1) | (p == 3))
        high = one * flag(p == 2) + two * flag(p >= 2) + three * flag(p == 3)
        return low.astype(BF), high.astype(BF)

    buckets = (
        pair(pos[Y], gy1, gy2, gy3) + pair(pos[Z], rz1, rz2, rz3) + pair(pos[X], gx1, gx2, gx3)
    )
    total = out_t[0]
    query = query_t[0]
    level_out[0, :9, :] = level_in[0, :9, :]
    for j, bucket in enumerate(buckets):
        row = mix[0, 9 + j : 10 + j, :] * scale_of(9 + j)
        reads = dot(bucket, qt, ((0,), (0,)))
        total = total + reads * row
        level_out[0, 9 + j : 10 + j, :] = jnp.sum(reads * gt, axis=0, keepdims=True) * scale_of(
            9 + j
        )
        query = query + dot(bucket, (gt * row).astype(BF), ((1,), (0,)))
    attended[...] = total.T.astype(BF)
    grads[0] = (query * DH**-0.5).T.astype(BF)


def column_kernel(pos, left, right, c0, c1, c2, c3, whole):
    whole[:, :1024] = left[...]
    whole[:, 1024:] = right[...]
    first = pos[3] == 0
    line = jnp.where(first, pos[X], pos[Z])
    for step, out in enumerate((c0, c1, c2, c3)):
        at = lax.rem(line + step, 4)
        for tile in range(4):
            column = jnp.where(first, 512 * at + 128 * tile, 512 * tile + 128 * at)
            out[:, 128 * tile : 128 * (tile + 1)] = whole[:, pl.ds(pl.multiple_of(column, 128), 128)]


def part(index):
    return pl.BlockSpec((1, 256, DH), lambda h: (index, 0, h))


COLUMNS = pl.BlockSpec((256, DH), lambda h: (0, h))
STATE = pl.BlockSpec((DH, DH), lambda h: (h, 0))
MIX = pl.BlockSpec((1, 15, 256), lambda h: (h, 0, 0))
TURNED = pl.BlockSpec((1, DH, 256), lambda h: (h, 0, 0))
SCALARS = pl.BlockSpec(memory_space=pltpu.SMEM)


def shape(dims, kind):
    return jax.ShapeDtypeStruct(dims, kind)


def layer(hidden, proj_weights, level_mix, out_grad):
    x, z, y = (lax.axis_index(name) for name in SEQ)
    core = lax.axis_index("head")
    first = core == 0
    pos = jnp.stack([x, z, y, core]).astype(jnp.int32)
    other = partner(hidden)
    left, right = jnp.where(first, hidden, other), jnp.where(first, other, hidden)
    root = jnp.array([DH**-0.5, 1.0, 1.0], F32)[:, None, None]
    near = lax.dynamic_slice_in_dim(proj_weights, 1024 * core, 1024, 0)
    far = lax.dynamic_slice_in_dim(proj_weights, 1024 * (1 - core), 1024, 0)
    near_part = jnp.einsum("td,dme->mte", hidden, near, preferred_element_type=F32)
    far_part = jnp.einsum("td,dme->mte", other, far, preferred_element_type=F32)
    projected = ((near_part + far_part) * root).astype(BF)
    mix = level_mix.transpose(1, 0, 2)

    whole = pl.BlockSpec(memory_space=pltpu.VMEM)
    own_columns, *far_columns = pl.pallas_call(
        column_kernel,
        in_specs=[SCALARS, whole, whole],
        out_specs=[whole] * 4,
        out_shape=[shape((256, 512), BF)] * 4,
        scratch_shapes=[pltpu.VMEM((256, 2048), BF)],
    )(pos, left, right)
    hidden_blocks = [own_columns]
    for n, block in zip((1, 2, 3), far_columns):
        hidden_blocks.append(shifted(block, (X, Z), n))

    state_shape = shape((512, DH), BF)
    states, b0, b1, b2, b3, b5, u3 = pl.pallas_call(
        state_kernel,
        name="state",
        grid=(4,),
        in_specs=[SCALARS, part(0), part(1), part(2), COLUMNS, MIX],
        out_specs=[STATE] * 7,
        out_shape=[state_shape] * 7,
    )(pos, projected, projected, projected, out_grad, mix)

    def line_of(axis):
        return (axis, axis)

    def sent(pieces, axis, which="all"):
        out = []
        for n, piece in zip((1, 2, 3), pieces):
            out.append(shifted(piece, line_of(axis), n, which))
        return out

    gy = sent([states] * 3, Y)
    rx = sent([b5, b5, u3], X, "down")
    inner_call = pl.pallas_call(
        inner_kernel,
        name="inner",
        grid=(4,),
        in_specs=[part(0), part(1), part(2), COLUMNS, MIX],
        out_specs=[
            TURNED,
            TURNED,
            COLUMNS,
            COLUMNS,
            pl.BlockSpec((1, 16, 256), lambda h: (h, 0, 0)),
        ],
        out_shape=[
            shape((4, DH, 256), F32),
            shape((4, DH, 256), F32),
            shape((256, 512), F32),
            shape((256, 512), F32),
            shape((4, 16, 256), F32),
        ],
        scratch_shapes=[pltpu.VMEM((256, 256), jnp.int32)],
    )
    out_t, query_t, key_in, value_in, level_in = inner_call(
        projected, projected, projected, out_grad, mix
    )
    middle_call = pl.pallas_call(
        middle_kernel,
        name="middle",
        in_specs=[SCALARS] + [whole] * 9,
        out_specs=[whole] * 4,
        out_shape=[shape((1024, DH), BF)] * 3 + [shape((512, DH), F32)],
    )
    p1, p2, p3, held = middle_call(pos, states, *gy, *rx, b2, b3)
    rz = sent([p1, p2, p3], Z)
    late_call = pl.pallas_call(
        late_kernel,
        name="late",
        in_specs=[SCALARS] + [whole] * 7,
        out_specs=[whole] * 5,
        out_shape=[state_shape] * 4 + [shape((512, DH), F32)],
    )
    group, q1, q2, q3, held = late_call(pos, p1, *rz, held, b0, b1)
    gx = sent([group] * 3, X, "up")
    ry = sent([q1, q2, q3], Y)
    grads = [None, None]
    grads[0] = pl.pallas_call(
        key_value_kernel,
        grid=(4,),
        in_specs=[part(1), part(2), COLUMNS, COLUMNS] + [STATE] * 4,
        out_specs=pl.BlockSpec((2, 256, DH), lambda h: (0, 0, h)),
        out_shape=shape((2, 256, 512), BF),
    )(projected, projected, key_in, value_in, held, *ry)
    attended, grads[1], level_grad = pl.pallas_call(
        query_kernel,
        grid=(4,),
        in_specs=[SCALARS, part(0), COLUMNS, MIX, TURNED, TURNED]
        + [pl.BlockSpec((1, 16, 256), lambda h: (h, 0, 0))]
        + [STATE] * 9,
        out_specs=[COLUMNS, part(0), MIX],
        out_shape=[
            shape((256, 512), BF),
            shape((1, 256, 512), BF),
            shape((4, 15, 256), F32),
        ],
    )(pos, projected, out_grad, mix, out_t, query_t, level_in, *gy, *rz, *gx)
    level_grad = level_grad.transpose(1, 0, 2)

    grad_blocks = [[grads[0]], [grads[1]]]
    for i in (0, 1):
        for n in (1, 2, 3):
            grad_blocks[i].append(shifted(grads[i], (X, Z), n))

    all_grads = jnp.concatenate([grads[1], grads[0]], axis=0)
    partial_inputs = jnp.einsum("mte,dme->td", all_grads, proj_weights, preferred_element_type=F32)
    mine = lax.dynamic_slice_in_dim(partial_inputs, 1024 * core, 1024, 1)
    theirs = lax.dynamic_slice_in_dim(partial_inputs, 1024 * (1 - core), 1024, 1)
    came = partner(theirs)
    input_grad = (mine + came).astype(BF)

    def products(blocks):
        return functools.reduce(
            jnp.add,
            [
                jnp.einsum("td,mte->mde", h, g, preferred_element_type=F32)
                for h, g in zip(hidden_blocks, blocks)
            ],
        )

    key_value_products = products(grad_blocks[0])
    query_products = products(grad_blocks[1])
    partial_weights = jnp.concatenate([query_products, key_value_products], axis=0)

    def reduced(array, at, axes, rows):
        def rows_of(step):
            return lax.dynamic_slice_in_dim(array, rows * ((at + step) % 4), rows, 1)

        came = []
        for n in (1, 2, 3):
            came.append(shifted(rows_of(n).astype(BF), axes, n))
        return rows_of(0) + came[0] + came[1] + came[2]

    partial_weights = reduced(partial_weights, jnp.where(first, z, x), (Z, X), 128)
    partial_weights = reduced(partial_weights, y, (Y, Y), 32)
    weight_grad = (partial_weights * 16384**-0.5).transpose(1, 0, 2)
    return (attended, input_grad, weight_grad, level_grad)


def solution(mesh):
    split = Mesh(mesh.devices.reshape(4, 4, 4, 2), ALL)
    return jax.shard_map(
        layer,
        mesh=split,
        in_specs=(P(SEQ, "head"), P(None, None, "head"), P(None, "head", SEQ), P(SEQ, "head")),
        out_specs=(P(SEQ, "head"), P(SEQ, "head"), P(SEQ, None, "head"), P(None, "head", SEQ)),
        check_vma=False,
    )
```

```python
import functools

import jax
import jax.numpy as jnp
from jax import lax
from jax.experimental import pallas as pl
from jax.experimental.pallas import tpu as pltpu
from jax.sharding import Mesh
from jax.sharding import PartitionSpec as P


DH = 128
SEQ = ("seq_0", "seq_1", "seq_2")
ALL = SEQ + ("head",)
BF = jnp.bfloat16
F32 = jnp.float32
X, Z, Y = 0, 1, 2


def scale_of(level):
    return 1.0 if level == 0 else 2.0 ** (-(level - 1) / 2)


def places():
    return [
        (x, z, y, h) for x in range(4) for z in range(4) for y in range(4) for h in range(2)
    ]


def index_of(place):
    x, z, y, h = place
    return ((x * 4 + z) * 4 + y) * 2 + h


def shifted(value, axes, step, which="all"):
    pairs = []
    for place in places():
        axis = axes[place[3]]
        target = list(place)
        target[axis] = (place[axis] + step) % 4
        if which == "up" and target[axis] < place[axis]:
            continue
        if which == "down" and target[axis] > place[axis]:
            continue
        pairs.append((index_of(place), index_of(target)))
    return lax.ppermute(value, ALL, pairs)


def partner(value):
    return lax.ppermute(value, "head", [(0, 1), (1, 0)])


def dot(a, b, dims):
    return lax.dot_general(a, b, (dims, ((), ())), preferred_element_type=F32)


def flag(condition):
    return jnp.where(condition, 1.0, 0.0).astype(F32)


def turned(array):
    return array.astype(F32).T


def heads():
    return [(h, slice(h * DH, (h + 1) * DH)) for h in range(4)]


def state_kernel(pos, proj, grads, mix, s_out, b0, b1, b2, b3, b5, u3):
    two = flag(pos[X] == 2)
    for h, cols in heads():
        qt = turned(proj[0, :, cols])
        kt = turned(proj[1, :, cols]).astype(BF)
        gg = grads[:, cols]
        s_out[cols, :] = dot(kt, proj[2, :, cols], ((1,), (0,))).astype(BF)

        def grad(j):
            row = mix[h, 9 + j : 10 + j, :] * scale_of(9 + j)
            return dot((qt * row).astype(BF), gg, ((1,), (0,)))

        b0[cols, :] = grad(0).astype(BF)
        b1[cols, :] = grad(1).astype(BF)
        b2[cols, :] = grad(2).astype(BF)
        b3[cols, :] = grad(3).astype(BF)
        g4, g5 = grad(4), grad(5)
        b5[cols, :] = g5.astype(BF)
        u3[cols, :] = (g5 * two + g4 * (1.0 - two)).astype(BF)


def up_terms(p, low, high):
    one = high * flag(p == 3)
    two = high * flag(p >= 2)
    three = low * flag((p == 1) | (p == 3)) + high * flag(p == 2)
    return one, two, three


def middle_kernel(pos, s, gy1, gy2, gy3, r1, r2, r3, b2, b3, p1, p2, p3, held):
    group = s[...].astype(F32) + gy1[...] + gy2[...] + gy3[...]
    held_now = r1[...].astype(F32) + r2[...] + r3[...]
    held[...] = held_now
    terms = up_terms(pos[Z], b2[...].astype(F32), b3[...].astype(F32))
    group = group.astype(BF)
    for out, term in zip((p1, p2, p3), terms):
        out[:512] = group
        out[512:] = (held_now + term).astype(BF)


def late_kernel(pos, p1, rz1, rz2, rz3, held, b0, b1, group, q1, q2, q3, held_out):
    whole = p1[:512].astype(F32) + rz1[:512] + rz2[:512] + rz3[:512]
    group[...] = whole.astype(BF)
    held_now = held[...] + rz1[512:].astype(F32) + rz2[512:] + rz3[512:]
    held_out[...] = held_now
    terms = up_terms(pos[Y], b0[...].astype(F32), b1[...].astype(F32))
    for out, term in zip((q1, q2, q3), terms):
        out[...] = (held_now + term).astype(BF)


def inner_kernel(proj, grads, mix, out_t, query_t, key_out, value_out, level_out, table):
    s_at = lax.broadcasted_iota(jnp.int32, (256, 256), 0)
    t_at = lax.broadcasted_iota(jnp.int32, (256, 256), 1)
    apart = s_at ^ t_at
    level = jnp.zeros((256, 256), jnp.int32)
    for place in range(8):
        level = level + (apart >= (1 << place)).astype(jnp.int32)
    table[...] = jnp.where(s_at <= t_at, level, -1)

    def one_head(h, _):
        cols = pl.ds(pl.multiple_of(h * DH, DH), DH)
        qq, kk, vv, gg = proj[0, :, cols], proj[1, :, cols], proj[2, :, cols], grads[:, cols]
        kt = turned(kk).astype(BF)
        vt = turned(vv).astype(BF)
        scores = dot(kk, qq, ((1,), (1,)))
        mix_grad = dot(vv, gg, ((1,), (1,)))
        levels = table[...]
        weight = jnp.zeros((256, 256), F32)
        product = scores * mix_grad
        for level in range(9):
            here = levels == level
            weight = jnp.where(here, mix[h, level : level + 1, :] * scale_of(level), weight)
            level_out[h, level : level + 1, :] = jnp.sum(
                jnp.where(here, product, 0.0), axis=0, keepdims=True
            ) * scale_of(level)
        mixed = (weight * scores).astype(BF)
        score_grad = (weight * mix_grad).astype(BF)
        out_t[h] = dot(vt, mixed, ((1,), (0,)))
        query_t[h] = dot(kt, score_grad, ((1,), (0,)))
        key_out[:, cols] = dot(score_grad, qq, ((1,), (0,)))
        value_out[:, cols] = dot(mixed, gg, ((1,), (0,)))
        return 0

    lax.fori_loop(0, 4, one_head, 0)


def key_value_kernel(proj, key_in, value_in, held, ry1, ry2, ry3, grads):
    for _, cols in heads():
        state = held[cols, :] + ry1[cols, :].astype(F32) + ry2[cols, :] + ry3[cols, :]
        state = state.astype(BF)
        grads[0, :, cols] = (key_in[:, cols] + dot(proj[2, :, cols], state, ((1,), (1,)))).astype(
            BF
        )
        grads[1, :, cols] = (
            value_in[:, cols] + dot(proj[1, :, cols], state, ((1,), (0,)))
        ).astype(BF)


def query_kernel(
    pos, proj, out_grad, mix, out_t, query_t, level_in, gy1, gy2, gy3, rz1, rz2, rz3, gx1, gx2,
    gx3, attended, grads, level_out,
):
    for h, cols in heads():
        qt = turned(proj[0, :, cols]).astype(BF)
        gt = turned(out_grad[:, cols])

        def pair(p, *parts):
            one, two, three = (a[cols, :].astype(F32) for a in parts)
            low = one * flag((p == 1) | (p == 3))
            high = one * flag(p == 2) + two * flag(p >= 2) + three * flag(p == 3)
            return low.astype(BF), high.astype(BF)

        buckets = (
            pair(pos[Y], gy1, gy2, gy3) + pair(pos[Z], rz1, rz2, rz3) + pair(pos[X], gx1, gx2, gx3)
        )
        total = out_t[h]
        query = query_t[h]
        level_out[h, :9, :] = level_in[h, :9, :]
        for j, bucket in enumerate(buckets):
            row = mix[h, 9 + j : 10 + j, :] * scale_of(9 + j)
            reads = dot(bucket, qt, ((0,), (0,)))
            total = total + reads * row
            level_out[h, 9 + j : 10 + j, :] = jnp.sum(
                reads * gt, axis=0, keepdims=True
            ) * scale_of(9 + j)
            query = query + dot(bucket, (gt * row).astype(BF), ((1,), (0,)))
        attended[:, cols] = total.T.astype(BF)
        grads[0, :, cols] = (query * DH**-0.5).T.astype(BF)


def column_kernel(pos, hidden, other, c0, c1, c2, c3, whole):
    core = pos[3]
    whole[:, pl.ds(pl.multiple_of(core * 1024, 1024), 1024)] = hidden[...]
    whole[:, pl.ds(pl.multiple_of((1 - core) * 1024, 1024), 1024)] = other[...]
    line = jnp.where(core == 0, pos[X], pos[Z])
    for step, out in enumerate((c0, c1, c2, c3)):
        at = lax.rem(line + step, 4)
        for tile in range(4):
            column = jnp.where(core == 0, 512 * at + 128 * tile, 512 * tile + 128 * at)
            out[:, 128 * tile : 128 * (tile + 1)] = whole[:, pl.ds(pl.multiple_of(column, 128), 128)]


def second_kernel(pos, query, key_value, own, o1, o2, o3):
    line = jnp.where(pos[3] == 0, pos[Z], pos[X])
    for step, out in enumerate((own, o1, o2, o3)):
        rows = pl.ds(pl.multiple_of(lax.rem(line + step, 4) * 128, 128), 128)
        out[0] = query[0, rows, :].astype(out.dtype)
        out[1] = key_value[0, rows, :].astype(out.dtype)
        out[2] = key_value[1, rows, :].astype(out.dtype)


def third_kernel(pos, mine, came1, came2, came3, own, o1, o2, o3, total):
    total[...] = mine[...] + came1[...].astype(F32) + came2[...] + came3[...]
    for step, out in enumerate((own, o1, o2, o3)):
        rows = pl.ds(pl.multiple_of(lax.rem(pos[Y] + step, 4) * 32, 32), 32)
        out[...] = total[:, rows, :].astype(out.dtype)


def shape(dims, kind):
    return pltpu.VMEM(dims, kind)


def call(kernel, arrays, outs, pos=None, scratch=()):
    whole = pl.BlockSpec(memory_space=pltpu.VMEM)
    scalars = [] if pos is None else [pl.BlockSpec(memory_space=pltpu.SMEM)]
    run = pl.pallas_call(
        kernel,
        in_specs=scalars + [whole] * len(arrays),
        out_specs=[whole] * len(outs),
        out_shape=outs,
        scratch_shapes=scratch,
        compiler_params=pltpu.CompilerParams(vmem_limit_bytes=8 << 20),
    )
    held = [pltpu.with_memory_space_constraint(a, pltpu.VMEM) for a in arrays]
    return run(*([] if pos is None else [pos]), *held)


def layer(hidden, proj_weights, level_mix, out_grad):
    x, z, y = (lax.axis_index(name) for name in SEQ)
    core = lax.axis_index("head")
    pos = jnp.stack([x, z, y, core]).astype(jnp.int32)
    other = partner(hidden)
    root = jnp.array([DH**-0.5, 1.0, 1.0], F32)[:, None, None]
    near = lax.dynamic_slice_in_dim(proj_weights, 1024 * core, 1024, 0)
    far = lax.dynamic_slice_in_dim(proj_weights, 1024 * (1 - core), 1024, 0)
    near_part = jnp.einsum("td,dme->mte", hidden, near, preferred_element_type=F32)
    far_part = jnp.einsum("td,dme->mte", other, far, preferred_element_type=F32)
    projected = ((near_part + far_part) * root).astype(BF)
    mix = level_mix.transpose(1, 0, 2)

    own_columns, *far_columns = call(
        column_kernel,
        [hidden, other],
        [shape((256, 512), BF)] * 4,
        pos,
        [pltpu.VMEM((256, 2048), BF)],
    )
    hidden_blocks = [own_columns]
    for n, block in zip((1, 2, 3), far_columns):
        hidden_blocks.append(shifted(block, (X, Z), n))

    state_shape = shape((512, DH), BF)
    states, b0, b1, b2, b3, b5, u3 = call(
        state_kernel, [projected, out_grad, mix], [state_shape] * 7, pos
    )

    def line_of(axis):
        return (axis, axis)

    def sent(pieces, axis, which="all"):
        out = []
        for n, piece in zip((1, 2, 3), pieces):
            out.append(shifted(piece, line_of(axis), n, which))
        return out

    gy = sent([states] * 3, Y)
    rx = sent([b5, b5, u3], X, "down")
    out_t, query_t, key_in, value_in, level_in = call(
        inner_kernel,
        [projected, out_grad, mix],
        [shape((4, DH, 256), F32)] * 2
        + [shape((256, 512), F32)] * 2
        + [shape((4, 16, 256), F32)],
        scratch=[pltpu.VMEM((256, 256), jnp.int32)],
    )
    p1, p2, p3, held = call(
        middle_kernel,
        [states, *gy, *rx, b2, b3],
        [shape((1024, DH), BF)] * 3 + [shape((512, DH), F32)],
        pos,
    )
    rz = sent([p1, p2, p3], Z)
    group, q1, q2, q3, held = call(
        late_kernel, [p1, *rz, held, b0, b1], [state_shape] * 4 + [shape((512, DH), F32)], pos
    )
    gx = sent([group] * 3, X, "up")
    ry = sent([q1, q2, q3], Y)
    grads = [None, None]
    (grads[0],) = call(
        key_value_kernel, [projected, key_in, value_in, held, *ry], [shape((2, 256, 512), BF)]
    )
    attended, grads[1], level_grad = call(
        query_kernel,
        [projected, out_grad, mix, out_t, query_t, level_in, *gy, *rz, *gx],
        [shape((256, 512), BF), shape((1, 256, 512), BF), shape((4, 15, 256), F32)],
        pos,
    )
    level_grad = level_grad.transpose(1, 0, 2)

    grad_blocks = [[grads[0]], [grads[1]]]
    for i in (0, 1):
        for n in (1, 2, 3):
            grad_blocks[i].append(shifted(grads[i], (X, Z), n))

    all_grads = jnp.concatenate([grads[1], grads[0]], axis=0)
    theirs = jnp.einsum("mte,dme->td", all_grads, far, preferred_element_type=F32)
    mine = lax.optimization_barrier(
        jnp.einsum("mte,dme->td", all_grads, near, preferred_element_type=F32)
    )
    came = partner(theirs)
    input_grad = (mine + came).astype(BF)

    def products(blocks):
        return functools.reduce(
            jnp.add,
            [
                jnp.einsum("td,mte->mde", h, g, preferred_element_type=F32)
                for h, g in zip(hidden_blocks, blocks)
            ],
        )

    key_value_products = products(grad_blocks[0])
    query_products = products(grad_blocks[1])

    def exchanged(pieces, axes):
        came = []
        for n, piece in zip((1, 2, 3), pieces):
            came.append(shifted(piece, axes, n))
        return came

    own, *pieces = call(
        second_kernel,
        [query_products, key_value_products],
        [shape((3, 128, 512), F32)] + [shape((3, 128, 512), BF)] * 3,
        pos,
    )
    own, *pieces = call(
        third_kernel,
        [own, *exchanged(pieces, (Z, X))],
        [shape((3, 32, 512), F32)] + [shape((3, 32, 512), BF)] * 3,
        pos,
        [pltpu.VMEM((3, 128, 512), F32)],
    )
    came = exchanged(pieces, (Y, Y))
    partial_weights = own + came[0] + came[1] + came[2]
    weight_grad = (partial_weights * 16384**-0.5).transpose(1, 0, 2)
    return (attended, input_grad, weight_grad, level_grad)


def solution(mesh):
    split = Mesh(mesh.devices.reshape(4, 4, 4, 2), ALL)
    return jax.shard_map(
        layer,
        mesh=split,
        in_specs=(P(SEQ, "head"), P(None, None, "head"), P(None, "head", SEQ), P(SEQ, "head")),
        out_specs=(P(SEQ, "head"), P(SEQ, "head"), P(SEQ, None, "head"), P(None, "head", SEQ)),
        check_vma=False,
    )
```

```python
import functools

import jax
import jax.numpy as jnp
from jax import lax
from jax.experimental import pallas as pl
from jax.experimental.pallas import tpu as pltpu
from jax.sharding import Mesh
from jax.sharding import PartitionSpec as P


DH = 128
SEQ = ("seq_0", "seq_1", "seq_2")
ALL = SEQ + ("head",)
BF = jnp.bfloat16
F32 = jnp.float32
X, Z, Y = 0, 1, 2


def scale_of(level):
    return 1.0 if level == 0 else 2.0 ** (-(level - 1) / 2)


def places():
    return [
        (x, z, y, h) for x in range(4) for z in range(4) for y in range(4) for h in range(2)
    ]


def index_of(place):
    x, z, y, h = place
    return ((x * 4 + z) * 4 + y) * 2 + h


def shifted(value, axes, step, which="all"):
    pairs = []
    for place in places():
        axis = axes[place[3]]
        target = list(place)
        target[axis] = (place[axis] + step) % 4
        if which == "up" and target[axis] < place[axis]:
            continue
        if which == "down" and target[axis] > place[axis]:
            continue
        pairs.append((index_of(place), index_of(target)))
    return lax.ppermute(value, ALL, pairs)


def partner(value):
    return lax.ppermute(value, "head", [(0, 1), (1, 0)])


def dot(a, b, dims):
    return lax.dot_general(a, b, (dims, ((), ())), preferred_element_type=F32)


def flag(condition):
    return jnp.where(condition, 1.0, 0.0).astype(F32)


def turned(array):
    return array.astype(F32).T


def heads():
    return [(h, slice(h * DH, (h + 1) * DH)) for h in range(4)]


def state_kernel(pos, proj, grads, mix, s_out, b0, b1, b2, b3, b5, u3):
    two = flag(pos[X] == 2)
    for h, cols in heads():
        qt = turned(proj[0, :, cols])
        kt = turned(proj[1, :, cols]).astype(BF)
        gg = grads[:, cols]
        s_out[cols, :] = dot(kt, proj[2, :, cols], ((1,), (0,))).astype(BF)

        def grad(j):
            row = mix[h, 9 + j : 10 + j, :] * scale_of(9 + j)
            return dot((qt * row).astype(BF), gg, ((1,), (0,)))

        b0[cols, :] = grad(0).astype(BF)
        b1[cols, :] = grad(1).astype(BF)
        b2[cols, :] = grad(2).astype(BF)
        b3[cols, :] = grad(3).astype(BF)
        g4, g5 = grad(4), grad(5)
        b5[cols, :] = g5.astype(BF)
        u3[cols, :] = (g5 * two + g4 * (1.0 - two)).astype(BF)


def up_terms(p, low, high):
    one = high * flag(p == 3)
    two = high * flag(p >= 2)
    three = low * flag((p == 1) | (p == 3)) + high * flag(p == 2)
    return one, two, three


def gather_kernel(mine, a1, a2, a3, group):
    group[...] = (mine[...].astype(F32) + a1[...] + a2[...] + a3[...]).astype(BF)


def upper_kernel(pos, r1, r2, r3, b2, b3, p1, p2, p3, held):
    held_now = r1[...].astype(F32) + r2[...] + r3[...]
    held[...] = held_now
    terms = up_terms(pos[Z], b2[...].astype(F32), b3[...].astype(F32))
    for out, term in zip((p1, p2, p3), terms):
        out[...] = (held_now + term).astype(BF)


def lower_kernel(pos, r1, r2, r3, held, b0, b1, q1, q2, q3, held_out):
    held_now = held[...] + r1[...].astype(F32) + r2[...] + r3[...]
    held_out[...] = held_now
    terms = up_terms(pos[Y], b0[...].astype(F32), b1[...].astype(F32))
    for out, term in zip((q1, q2, q3), terms):
        out[...] = (held_now + term).astype(BF)


def inner_kernel(proj, grads, mix, out_t, query_t, key_out, value_out, level_out, table):
    s_at = lax.broadcasted_iota(jnp.int32, (256, 256), 0)
    t_at = lax.broadcasted_iota(jnp.int32, (256, 256), 1)
    apart = s_at ^ t_at
    level = jnp.zeros((256, 256), jnp.int32)
    for place in range(8):
        level = level + (apart >= (1 << place)).astype(jnp.int32)
    table[...] = jnp.where(s_at <= t_at, level, -1)

    def one_head(h, _):
        cols = pl.ds(pl.multiple_of(h * DH, DH), DH)
        qq, kk, vv, gg = proj[0, :, cols], proj[1, :, cols], proj[2, :, cols], grads[:, cols]
        kt = turned(kk).astype(BF)
        vt = turned(vv).astype(BF)
        scores = dot(kk, qq, ((1,), (1,)))
        mix_grad = dot(vv, gg, ((1,), (1,)))
        levels = table[...]
        weight = jnp.zeros((256, 256), F32)
        product = scores * mix_grad
        for level in range(9):
            here = levels == level
            weight = jnp.where(here, mix[h, level : level + 1, :] * scale_of(level), weight)
            level_out[h, level : level + 1, :] = jnp.sum(
                jnp.where(here, product, 0.0), axis=0, keepdims=True
            ) * scale_of(level)
        mixed = (weight * scores).astype(BF)
        score_grad = (weight * mix_grad).astype(BF)
        out_t[h] = dot(vt, mixed, ((1,), (0,)))
        query_t[h] = dot(kt, score_grad, ((1,), (0,)))
        key_out[:, cols] = dot(score_grad, qq, ((1,), (0,)))
        value_out[:, cols] = dot(mixed, gg, ((1,), (0,)))
        return 0

    lax.fori_loop(0, 4, one_head, 0)


def key_value_kernel(proj, key_in, value_in, held, ry1, ry2, ry3, grads):
    for _, cols in heads():
        state = held[cols, :] + ry1[cols, :].astype(F32) + ry2[cols, :] + ry3[cols, :]
        state = state.astype(BF)
        grads[0, :, cols] = (key_in[:, cols] + dot(proj[2, :, cols], state, ((1,), (1,)))).astype(
            BF
        )
        grads[1, :, cols] = (
            value_in[:, cols] + dot(proj[1, :, cols], state, ((1,), (0,)))
        ).astype(BF)


def query_kernel(
    pos, proj, out_grad, mix, out_t, query_t, level_in, gy1, gy2, gy3, rz1, rz2, rz3, gx1, gx2,
    gx3, attended, grads, level_out,
):
    for h, cols in heads():
        qt = turned(proj[0, :, cols]).astype(BF)
        gt = turned(out_grad[:, cols])

        def pair(p, *parts):
            one, two, three = (a[cols, :].astype(F32) for a in parts)
            low = one * flag((p == 1) | (p == 3))
            high = one * flag(p == 2) + two * flag(p >= 2) + three * flag(p == 3)
            return low.astype(BF), high.astype(BF)

        buckets = (
            pair(pos[Y], gy1, gy2, gy3) + pair(pos[Z], rz1, rz2, rz3) + pair(pos[X], gx1, gx2, gx3)
        )
        total = out_t[h]
        query = query_t[h]
        level_out[h, :9, :] = level_in[h, :9, :]
        for j, bucket in enumerate(buckets):
            row = mix[h, 9 + j : 10 + j, :] * scale_of(9 + j)
            reads = dot(bucket, qt, ((0,), (0,)))
            total = total + reads * row
            level_out[h, 9 + j : 10 + j, :] = jnp.sum(
                reads * gt, axis=0, keepdims=True
            ) * scale_of(9 + j)
            query = query + dot(bucket, (gt * row).astype(BF), ((1,), (0,)))
        attended[:, cols] = total.T.astype(BF)
        grads[0, :, cols] = (query * DH**-0.5).T.astype(BF)


def column_kernel(pos, hidden, other, c0, c1, c2, c3, whole):
    core = pos[3]
    outs = (c0, c1, c2, c3)

    @pl.when(core == 0)
    def _():
        whole[:, :1024] = hidden[...]
        whole[:, 1024:] = other[...]
        for step, out in enumerate(outs):
            column = lax.rem(pos[X] + step, 4) * 512
            out[...] = whole[:, pl.ds(pl.multiple_of(column, 512), 512)]

    @pl.when(core == 1)
    def _():
        source = lax.broadcasted_iota(jnp.int32, (512, 128), 0)
        target = lax.broadcasted_iota(jnp.int32, (512, 128), 1)
        start = (target // 32) * 128 + target % 32
        for step, out in enumerate(outs):
            run = lax.rem(pos[Y] + step, 4) * 32
            pick = jnp.where(source == start + run, 1.0, 0.0).astype(BF)
            for tile in range(4):
                half = other if tile < 2 else hidden
                piece = half[:, 512 * (tile % 2) : 512 * (tile % 2) + 512]
                out[:, 128 * tile : 128 * tile + 128] = dot(piece, pick, ((1,), (0,))).astype(BF)


def second_kernel(pos, product, own, o1, o2, o3):
    line = jnp.where(pos[3] == 0, pos[Z], pos[X])
    for step, out in enumerate((own, o1, o2, o3)):
        rows = pl.ds(pl.multiple_of(lax.rem(line + step, 4) * 128, 128), 128)
        out[...] = product[:, rows, :].astype(out.dtype)


def third_kernel(
    pos, mine0, mine1, a1, a2, a3, b1, b2, b3, own, o1, o2, o3, total
):
    total[0:1] = mine0[...] + a1[...].astype(F32) + a2[...] + a3[...]
    total[1:3] = mine1[...] + b1[...].astype(F32) + b2[...] + b3[...]
    line = jnp.where(pos[3] == 0, pos[Y], pos[Z])
    for step, out in enumerate((own, o1, o2, o3)):
        rows = pl.ds(pl.multiple_of(lax.rem(line + step, 4) * 32, 32), 32)
        out[...] = total[:, rows, :].astype(out.dtype)


def shape(dims, kind):
    return pltpu.VMEM(dims, kind)


def call(kernel, arrays, outs, pos=None, scratch=()):
    whole = pl.BlockSpec(memory_space=pltpu.VMEM)
    scalars = [] if pos is None else [pl.BlockSpec(memory_space=pltpu.SMEM)]
    run = pl.pallas_call(
        kernel,
        in_specs=scalars + [whole] * len(arrays),
        out_specs=[whole] * len(outs),
        out_shape=outs,
        scratch_shapes=scratch,
        compiler_params=pltpu.CompilerParams(vmem_limit_bytes=8 << 20),
    )
    held = [pltpu.with_memory_space_constraint(a, pltpu.VMEM) for a in arrays]
    return run(*([] if pos is None else [pos]), *held)


def layer(hidden, proj_weights, level_mix, out_grad):
    x, z, y = (lax.axis_index(name) for name in SEQ)
    core = lax.axis_index("head")
    pos = jnp.stack([x, z, y, core]).astype(jnp.int32)
    other = partner(hidden)
    root = jnp.array([DH**-0.5, 1.0, 1.0], F32)[:, None, None]
    near = lax.dynamic_slice_in_dim(proj_weights, 1024 * core, 1024, 0)
    far = lax.dynamic_slice_in_dim(proj_weights, 1024 * (1 - core), 1024, 0)
    near_part = jnp.einsum("td,dme->mte", hidden, near, preferred_element_type=F32)
    far_part = jnp.einsum("td,dme->mte", other, far, preferred_element_type=F32)
    projected = ((near_part + far_part) * root).astype(BF)
    mix = level_mix.transpose(1, 0, 2)

    own_columns, *far_columns = call(
        column_kernel,
        [hidden, other],
        [shape((256, 512), BF)] * 4,
        pos,
        [pltpu.VMEM((256, 2048), BF)],
    )
    hidden_blocks = [own_columns]
    for n, block in zip((1, 2, 3), far_columns):
        hidden_blocks.append(shifted(block, (X, Y), n))

    state_shape = shape((512, DH), BF)
    states, b0, b1, b2, b3, b5, u3 = call(
        state_kernel, [projected, out_grad, mix], [state_shape] * 7, pos
    )

    def line_of(axis):
        return (axis, axis)

    def sent(pieces, axis, which="all"):
        out = []
        for n, piece in zip((1, 2, 3), pieces):
            out.append(shifted(piece, line_of(axis), n, which))
        return out

    gy = sent([states] * 3, Y)
    rx = sent([b5, b5, u3], X, "down")
    out_t, query_t, key_in, value_in, level_in = call(
        inner_kernel,
        [projected, out_grad, mix],
        [shape((4, DH, 256), F32)] * 2
        + [shape((256, 512), F32)] * 2
        + [shape((4, 16, 256), F32)],
        scratch=[pltpu.VMEM((256, 256), jnp.int32)],
    )
    p1, p2, p3, held = call(
        upper_kernel, [*rx, b2, b3], [state_shape] * 3 + [shape((512, DH), F32)], pos
    )
    uz = sent([p1, p2, p3], Z)
    (group,) = call(gather_kernel, [states, *gy], [state_shape])
    rz = sent([group] * 3, Z)
    q1, q2, q3, held = call(
        lower_kernel, [*uz, held, b0, b1], [state_shape] * 3 + [shape((512, DH), F32)], pos
    )
    ry = sent([q1, q2, q3], Y)
    (group,) = call(gather_kernel, [group, *rz], [state_shape])
    gx = sent([group] * 3, X, "up")
    grads = [None, None]
    (grads[0],) = call(
        key_value_kernel, [projected, key_in, value_in, held, *ry], [shape((2, 256, 512), BF)]
    )
    attended, grads[1], level_grad = call(
        query_kernel,
        [projected, out_grad, mix, out_t, query_t, level_in, *gy, *rz, *gx],
        [shape((256, 512), BF), shape((1, 256, 512), BF), shape((4, 15, 256), F32)],
        pos,
    )
    level_grad = level_grad.transpose(1, 0, 2)

    grad_blocks = [[grads[0]], [grads[1]]]
    for i in (0, 1):
        for n in (1, 2, 3):
            grad_blocks[i].append(shifted(grads[i], (X, Y), n))

    all_grads = jnp.concatenate([grads[1], grads[0]], axis=0)
    theirs = jnp.einsum("mte,dme->td", all_grads, far, preferred_element_type=F32)
    mine = lax.optimization_barrier(
        jnp.einsum("mte,dme->td", all_grads, near, preferred_element_type=F32)
    )
    came = partner(theirs)
    input_grad = (mine + came).astype(BF)

    def products(blocks):
        return functools.reduce(
            jnp.add,
            [
                jnp.einsum("td,mte->mde", h, g, preferred_element_type=F32)
                for h, g in zip(hidden_blocks, blocks)
            ],
        )

    key_value_products = products(grad_blocks[0])
    query_products = products(grad_blocks[1])

    def exchanged(pieces, axes):
        came = []
        for n, piece in zip((1, 2, 3), pieces):
            came.append(shifted(piece, axes, n))
        return came

    def second(product):
        size = product.shape[0]
        own, *pieces = call(
            second_kernel,
            [product],
            [shape((size, 128, 512), F32)] + [shape((size, 128, 512), BF)] * 3,
            pos,
        )
        return own, exchanged(pieces, (Z, X))

    own1, came1 = second(key_value_products)
    own0, came0 = second(query_products)
    own, *pieces = call(
        third_kernel,
        [own0, own1, *came0, *came1],
        [shape((3, 32, 512), F32)] + [shape((3, 32, 512), BF)] * 3,
        pos,
        [pltpu.VMEM((3, 128, 512), F32)],
    )
    came = exchanged(pieces, (Y, Z))
    partial_weights = own + came[0] + came[1] + came[2]
    weight_grad = (partial_weights * 16384**-0.5).transpose(1, 0, 2)
    return (attended, input_grad, weight_grad, level_grad)


def solution(mesh):
    split = Mesh(mesh.devices.reshape(4, 4, 4, 2), ALL)
    return jax.shard_map(
        layer,
        mesh=split,
        in_specs=(P(SEQ, "head"), P(None, None, "head"), P(None, "head", SEQ), P(SEQ, "head")),
        out_specs=(P(SEQ, "head"), P(SEQ, "head"), P(SEQ, None, "head"), P(None, "head", SEQ)),
        check_vma=False,
    )
```

```python
import functools

import jax
import jax.numpy as jnp
from jax import lax
from jax.experimental import pallas as pl
from jax.experimental.pallas import tpu as pltpu
from jax.sharding import Mesh
from jax.sharding import PartitionSpec as P


DH = 128
SEQ = ("seq_0", "seq_1", "seq_2")
ALL = SEQ + ("head",)
BF = jnp.bfloat16
F32 = jnp.float32
X, Z, Y = 0, 1, 2


def scale_of(level):
    return 1.0 if level == 0 else 2.0 ** (-(level - 1) / 2)


def places():
    return [
        (x, z, y, h) for x in range(4) for z in range(4) for y in range(4) for h in range(2)
    ]


def index_of(place):
    x, z, y, h = place
    return ((x * 4 + z) * 4 + y) * 2 + h


def shifted(value, axes, step, which="all"):
    pairs = []
    for place in places():
        axis = axes[place[3]]
        target = list(place)
        target[axis] = (place[axis] + step) % 4
        if which == "up" and target[axis] < place[axis]:
            continue
        if which == "down" and target[axis] > place[axis]:
            continue
        pairs.append((index_of(place), index_of(target)))
    return lax.ppermute(value, ALL, pairs)


def partner(value):
    return lax.ppermute(value, "head", [(0, 1), (1, 0)])


def dot(a, b, dims):
    return lax.dot_general(a, b, (dims, ((), ())), preferred_element_type=F32)


def flag(condition):
    return jnp.where(condition, 1.0, 0.0).astype(F32)


def turned(array):
    return array.astype(F32).T


def heads():
    return [(h, slice(h * DH, (h + 1) * DH)) for h in range(4)]


def state_kernel(pos, proj, grads, mix, s_out, b0, b1, b2, b3, b5, u3):
    two = flag(pos[X] == 2)
    for h, cols in heads():
        qt = turned(proj[0, :, cols])
        kt = turned(proj[1, :, cols]).astype(BF)
        gg = grads[:, cols]
        s_out[cols, :] = dot(kt, proj[2, :, cols], ((1,), (0,))).astype(BF)

        def grad(j):
            row = mix[9 + j, h : h + 1, :] * scale_of(9 + j)
            return dot((qt * row).astype(BF), gg, ((1,), (0,)))

        b0[cols, :] = grad(0).astype(BF)
        b1[cols, :] = grad(1).astype(BF)
        b2[cols, :] = grad(2).astype(BF)
        b3[cols, :] = grad(3).astype(BF)
        g4, g5 = grad(4), grad(5)
        b5[cols, :] = g5.astype(BF)
        u3[cols, :] = (g5 * two + g4 * (1.0 - two)).astype(BF)


def up_terms(p, low, high):
    one = high * flag(p == 3)
    two = high * flag(p >= 2)
    three = low * flag((p == 1) | (p == 3)) + high * flag(p == 2)
    return one, two, three


def gather_kernel(mine, a1, a2, a3, group):
    group[...] = (mine[...].astype(F32) + a1[...] + a2[...] + a3[...]).astype(BF)


def upper_kernel(pos, r1, r2, r3, b2, b3, p1, p2, p3, held):
    held_now = r1[...].astype(F32) + r2[...] + r3[...]
    held[...] = held_now
    terms = up_terms(pos[Z], b2[...].astype(F32), b3[...].astype(F32))
    for out, term in zip((p1, p2, p3), terms):
        out[...] = (held_now + term).astype(BF)


def lower_kernel(pos, r1, r2, r3, held, b0, b1, q1, q2, q3, held_out):
    held_now = held[...] + r1[...].astype(F32) + r2[...] + r3[...]
    held_out[...] = held_now
    terms = up_terms(pos[Y], b0[...].astype(F32), b1[...].astype(F32))
    for out, term in zip((q1, q2, q3), terms):
        out[...] = (held_now + term).astype(BF)


def inner_kernel(
    proj, grads, mix, out_t, query_t, key_out, value_out, level_out, table, mixed, score_grad
):
    half = DH
    s_at = lax.broadcasted_iota(jnp.int32, (half, half), 0)
    t_at = lax.broadcasted_iota(jnp.int32, (half, half), 1)
    apart = s_at ^ t_at
    level = jnp.zeros((half, half), jnp.int32)
    for place in range(7):
        level = level + (apart >= (1 << place)).astype(jnp.int32)
    table[...] = jnp.where(s_at <= t_at, level, -1)
    mixed[half:, :half] = jnp.zeros((half, half), BF)
    score_grad[half:, :half] = jnp.zeros((half, half), BF)

    for h, cols in heads():
        qq, kk, vv, gg = proj[0, :, cols], proj[1, :, cols], proj[2, :, cols], grads[:, cols]
        kt = turned(kk).astype(BF)
        vt = turned(vv).astype(BF)
        scores = dot(kk, qq, ((1,), (1,)))
        mix_grad = dot(vv, gg, ((1,), (1,)))

        def row(level, at, h=h):
            return mix[level, h : h + 1, at : at + half] * scale_of(level)

        levels = table[...]
        for at in (0, half):
            score, grad = scores[at : at + half, at : at + half], mix_grad[at : at + half, at : at + half]
            product = score * grad
            weight = jnp.zeros((half, half), F32)
            for level in range(8):
                here = levels == level
                weight = jnp.where(here, row(level, at), weight)
                level_out[level, h : h + 1, at : at + half] = jnp.sum(
                    jnp.where(here, product, 0.0), axis=0, keepdims=True
                ) * scale_of(level)
            mixed[at : at + half, at : at + half] = (weight * score).astype(BF)
            score_grad[at : at + half, at : at + half] = (weight * grad).astype(BF)
        score, grad = scores[:half, half:], mix_grad[:half, half:]
        weight = row(8, half)
        level_out[8, h : h + 1, :half] = jnp.zeros((1, half), F32)
        level_out[8, h : h + 1, half:] = jnp.sum(score * grad, axis=0, keepdims=True) * scale_of(8)
        mixed[:half, half:] = (weight * score).astype(BF)
        score_grad[:half, half:] = (weight * grad).astype(BF)

        out_t[h] = dot(vt, mixed[...], ((1,), (0,)))
        query_t[h] = dot(kt, score_grad[...], ((1,), (0,)))
        key_out[:, cols] = dot(score_grad[...], qq, ((1,), (0,)))
        value_out[:, cols] = dot(mixed[...], gg, ((1,), (0,)))


def key_value_kernel(proj, key_in, value_in, held, ry1, ry2, ry3, grads):
    for _, cols in heads():
        state = held[cols, :] + ry1[cols, :].astype(F32) + ry2[cols, :] + ry3[cols, :]
        state = state.astype(BF)
        grads[0, :, cols] = (key_in[:, cols] + dot(proj[2, :, cols], state, ((1,), (1,)))).astype(
            BF
        )
        grads[1, :, cols] = (
            value_in[:, cols] + dot(proj[1, :, cols], state, ((1,), (0,)))
        ).astype(BF)


def pair_of(p, *parts):
    one, two, three = (a.astype(F32) for a in parts)
    low = one * flag((p == 1) | (p == 3))
    high = one * flag(p == 2) + two * flag(p >= 2) + three * flag(p == 3)
    return low.astype(BF), high.astype(BF)


def query_kernel(pos, out_grad, mix, query_t, *refs):
    parts, (grads, buckets) = refs[:9], refs[9:]
    for h, cols in heads():
        gt = turned(out_grad[:, cols])
        query = query_t[h]
        for line in range(3):
            three = (a[cols, :] for a in parts[3 * line : 3 * line + 3])
            for j, bucket in enumerate(pair_of(pos[(Y, Z, X)[line]], *three), 2 * line):
                buckets[j, cols, :] = bucket
                row = mix[9 + j, h : h + 1, :] * scale_of(9 + j)
                query = query + dot(bucket, (gt * row).astype(BF), ((1,), (0,)))
        grads[0, :, cols] = (query * DH**-0.5).T.astype(BF)


def read_kernel(proj, out_grad, mix, out_t, level_in, buckets, attended, level_out):
    level_out[:9] = level_in[...]
    for h, cols in heads():
        qt = turned(proj[0, :, cols]).astype(BF)
        gt = turned(out_grad[:, cols])
        total = out_t[h]
        for j in range(6):
            row = mix[9 + j, h : h + 1, :] * scale_of(9 + j)
            reads = dot(buckets[j, cols, :], qt, ((0,), (0,)))
            total = total + reads * row
            level_out[9 + j, h : h + 1, :] = jnp.sum(
                reads * gt, axis=0, keepdims=True
            ) * scale_of(9 + j)
        attended[:, cols] = total.T.astype(BF)


def column_kernel(pos, hidden, other, c0, c1, c2, c3, whole):
    core = pos[3]
    outs = (c0, c1, c2, c3)

    @pl.when(core == 0)
    def _():
        whole[:, :1024] = hidden[...]
        whole[:, 1024:] = other[...]
        for step, out in enumerate(outs):
            column = lax.rem(pos[X] + step, 4) * 512
            out[...] = whole[:, pl.ds(pl.multiple_of(column, 512), 512)]

    @pl.when(core == 1)
    def _():
        source = lax.broadcasted_iota(jnp.int32, (512, 128), 0)
        target = lax.broadcasted_iota(jnp.int32, (512, 128), 1)
        start = (target // 32) * 128 + target % 32
        for step, out in enumerate(outs):
            run = lax.rem(pos[Y] + step, 4) * 32
            pick = jnp.where(source == start + run, 1.0, 0.0).astype(BF)
            for tile in range(4):
                half = other if tile < 2 else hidden
                piece = half[:, 512 * (tile % 2) : 512 * (tile % 2) + 512]
                out[:, 128 * tile : 128 * tile + 128] = dot(piece, pick, ((1,), (0,))).astype(BF)


def second_kernel(pos, product, own, o1, o2, o3):
    line = jnp.where(pos[3] == 0, pos[Z], pos[X])
    for step, out in enumerate((own, o1, o2, o3)):
        rows = pl.ds(pl.multiple_of(lax.rem(line + step, 4) * 128, 128), 128)
        out[...] = product[:, rows, :].astype(out.dtype)


def third_kernel(
    pos, mine0, mine1, a1, a2, a3, b1, b2, b3, own, o1, o2, o3, total
):
    total[0:1] = mine0[...] + a1[...].astype(F32) + a2[...] + a3[...]
    total[1:3] = mine1[...] + b1[...].astype(F32) + b2[...] + b3[...]
    line = jnp.where(pos[3] == 0, pos[Y], pos[Z])
    for step, out in enumerate((own, o1, o2, o3)):
        rows = pl.ds(pl.multiple_of(lax.rem(line + step, 4) * 32, 32), 32)
        out[...] = total[:, rows, :].astype(out.dtype)


def shape(dims, kind):
    return pltpu.VMEM(dims, kind)


def call(kernel, arrays, outs, pos=None, scratch=()):
    whole = pl.BlockSpec(memory_space=pltpu.VMEM)
    scalars = [] if pos is None else [pl.BlockSpec(memory_space=pltpu.SMEM)]
    run = pl.pallas_call(
        kernel,
        in_specs=scalars + [whole] * len(arrays),
        out_specs=[whole] * len(outs),
        out_shape=outs,
        scratch_shapes=scratch,
        compiler_params=pltpu.CompilerParams(vmem_limit_bytes=8 << 20),
    )
    held = [pltpu.with_memory_space_constraint(a, pltpu.VMEM) for a in arrays]
    return run(*([] if pos is None else [pos]), *held)


def layer(hidden, proj_weights, level_mix, out_grad):
    x, z, y = (lax.axis_index(name) for name in SEQ)
    core = lax.axis_index("head")
    pos = jnp.stack([x, z, y, core]).astype(jnp.int32)
    other = partner(hidden)
    root = jnp.array([DH**-0.5, 1.0, 1.0], F32)[:, None, None]
    near = lax.dynamic_slice_in_dim(proj_weights, 1024 * core, 1024, 0)
    far = lax.dynamic_slice_in_dim(proj_weights, 1024 * (1 - core), 1024, 0)
    near_part = jnp.einsum("td,dme->mte", hidden, near, preferred_element_type=F32)
    far_part = jnp.einsum("td,dme->mte", other, far, preferred_element_type=F32)
    projected = ((near_part + far_part) * root).astype(BF)
    mix = level_mix

    own_columns, *far_columns = call(
        column_kernel,
        [hidden, other],
        [shape((256, 512), BF)] * 4,
        pos,
        [pltpu.VMEM((256, 2048), BF)],
    )
    hidden_blocks = [own_columns]
    for n, block in zip((1, 2, 3), far_columns):
        hidden_blocks.append(shifted(block, (X, Y), n))

    state_shape = shape((512, DH), BF)
    states, b0, b1, b2, b3, b5, u3 = call(
        state_kernel, [projected, out_grad, mix], [state_shape] * 7, pos
    )

    def line_of(axis):
        return (axis, axis)

    def sent(pieces, axis, which="all"):
        out = []
        for n, piece in zip((1, 2, 3), pieces):
            out.append(shifted(piece, line_of(axis), n, which))
        return out

    gy = sent([states] * 3, Y)
    rx = sent([b5, b5, u3], X, "down")
    out_t, query_t, key_in, value_in, level_in = call(
        inner_kernel,
        [projected, out_grad, mix],
        [shape((4, DH, 256), F32)] * 2
        + [shape((256, 512), F32)] * 2
        + [shape((9, 4, 256), F32)],
        scratch=[pltpu.VMEM((DH, DH), jnp.int32)] + [pltpu.VMEM((256, 256), BF)] * 2,
    )
    p1, p2, p3, held = call(
        upper_kernel, [*rx, b2, b3], [state_shape] * 3 + [shape((512, DH), F32)], pos
    )
    uz = sent([p1, p2, p3], Z)
    (group,) = call(gather_kernel, [states, *gy], [state_shape])
    rz = sent([group] * 3, Z)
    q1, q2, q3, held = call(
        lower_kernel, [*uz, held, b0, b1], [state_shape] * 3 + [shape((512, DH), F32)], pos
    )
    ry = sent([q1, q2, q3], Y)
    (group,) = call(gather_kernel, [group, *rz], [state_shape])
    gx = sent([group] * 3, X, "up")
    grads = [None, None]
    (grads[0],) = call(
        key_value_kernel, [projected, key_in, value_in, held, *ry], [shape((2, 256, 512), BF)]
    )
    grads[1], buckets = call(
        query_kernel,
        [out_grad, mix, query_t, *gy, *rz, *gx],
        [shape((1, 256, 512), BF), shape((6, 512, DH), BF)],
        pos,
    )
    attended, level_grad = call(
        read_kernel,
        [projected, out_grad, mix, out_t, level_in, buckets],
        [shape((256, 512), BF), shape((15, 4, 256), F32)],
    )

    grad_blocks = [[grads[0]], [grads[1]]]
    for i in (0, 1):
        for n in (1, 2, 3):
            grad_blocks[i].append(shifted(grads[i], (X, Y), n))

    all_grads = jnp.concatenate([grads[1], grads[0]], axis=0)
    theirs = jnp.einsum("mte,dme->td", all_grads, far, preferred_element_type=F32)
    mine = lax.optimization_barrier(
        jnp.einsum("mte,dme->td", all_grads, near, preferred_element_type=F32)
    )
    came = partner(theirs)
    input_grad = (mine + came).astype(BF)

    def products(blocks):
        return functools.reduce(
            jnp.add,
            [
                jnp.einsum("td,mte->mde", h, g, preferred_element_type=F32)
                for h, g in zip(hidden_blocks, blocks)
            ],
        )

    key_value_products = products(grad_blocks[0])
    query_products = products(grad_blocks[1])

    def exchanged(pieces, axes):
        came = []
        for n, piece in zip((1, 2, 3), pieces):
            came.append(shifted(piece, axes, n))
        return came

    def second(product):
        size = product.shape[0]
        own, *pieces = call(
            second_kernel,
            [product],
            [shape((size, 128, 512), F32)] + [shape((size, 128, 512), BF)] * 3,
            pos,
        )
        return own, exchanged(pieces, (Z, X))

    own1, came1 = second(key_value_products)
    own0, came0 = second(query_products)
    own, *pieces = call(
        third_kernel,
        [own0, own1, *came0, *came1],
        [shape((3, 32, 512), F32)] + [shape((3, 32, 512), BF)] * 3,
        pos,
        [pltpu.VMEM((3, 128, 512), F32)],
    )
    came = exchanged(pieces, (Y, Z))
    partial_weights = own + came[0] + came[1] + came[2]
    weight_grad = (partial_weights * 16384**-0.5).transpose(1, 0, 2)
    return (attended, input_grad, weight_grad, level_grad)


def solution(mesh):
    split = Mesh(mesh.devices.reshape(4, 4, 4, 2), ALL)
    return jax.shard_map(
        layer,
        mesh=split,
        in_specs=(P(SEQ, "head"), P(None, None, "head"), P(None, "head", SEQ), P(SEQ, "head")),
        out_specs=(P(SEQ, "head"), P(SEQ, "head"), P(SEQ, None, "head"), P(None, "head", SEQ)),
        check_vma=False,
    )
```

```python
import functools

import jax
import jax.numpy as jnp
from jax import lax
from jax.experimental import pallas as pl
from jax.experimental.pallas import tpu as pltpu
from jax.sharding import Mesh
from jax.sharding import PartitionSpec as P


DH = 128
SEQ = ("seq_0", "seq_1", "seq_2")
ALL = SEQ + ("head",)
BF = jnp.bfloat16
F32 = jnp.float32
X, Z, Y = 0, 1, 2


def scale_of(level):
    return 1.0 if level == 0 else 2.0 ** (-(level - 1) / 2)


def places():
    return [
        (x, z, y, h) for x in range(4) for z in range(4) for y in range(4) for h in range(2)
    ]


def index_of(place):
    x, z, y, h = place
    return ((x * 4 + z) * 4 + y) * 2 + h


def shifted(value, axes, step, which="all"):
    pairs = []
    for place in places():
        axis = axes[place[3]]
        target = list(place)
        target[axis] = (place[axis] + step) % 4
        if which == "up" and target[axis] < place[axis]:
            continue
        if which == "down" and target[axis] > place[axis]:
            continue
        pairs.append((index_of(place), index_of(target)))
    return lax.ppermute(value, ALL, pairs)


def partner(value):
    return lax.ppermute(value, "head", [(0, 1), (1, 0)])


def dot(a, b, dims):
    return lax.dot_general(a, b, (dims, ((), ())), preferred_element_type=F32)


def flag(condition):
    return jnp.where(condition, 1.0, 0.0).astype(F32)


def turned(array):
    return array.astype(F32).T


def heads():
    return [(h, slice(h * DH, (h + 1) * DH)) for h in range(4)]


def state_kernel(pos, proj, grads, mix, s_out, b0, b1, b2, b3, b5, u3):
    two = flag(pos[X] == 2)
    for h, cols in heads():
        qt = turned(proj[0, :, cols])
        kt = turned(proj[1, :, cols]).astype(BF)
        gg = grads[:, cols]
        s_out[cols, :] = dot(kt, proj[2, :, cols], ((1,), (0,))).astype(BF)

        def grad(j):
            row = mix[9 + j, h : h + 1, :] * scale_of(9 + j)
            return dot((qt * row).astype(BF), gg, ((1,), (0,)))

        b0[cols, :] = grad(0).astype(BF)
        b1[cols, :] = grad(1).astype(BF)
        b2[cols, :] = grad(2).astype(BF)
        b3[cols, :] = grad(3).astype(BF)
        g4, g5 = grad(4), grad(5)
        b5[cols, :] = g5.astype(BF)
        u3[cols, :] = (g5 * two + g4 * (1.0 - two)).astype(BF)


def up_terms(p, low, high):
    one = high * flag(p == 3)
    two = high * flag(p >= 2)
    three = low * flag((p == 1) | (p == 3)) + high * flag(p == 2)
    return one, two, three


def gather_kernel(mine, a1, a2, a3, group):
    group[...] = (mine[...].astype(F32) + a1[...] + a2[...] + a3[...]).astype(BF)


def upper_kernel(pos, r1, r2, r3, b2, b3, p1, p2, p3, held):
    held_now = r1[...].astype(F32) + r2[...] + r3[...]
    held[...] = held_now
    terms = up_terms(pos[Z], b2[...].astype(F32), b3[...].astype(F32))
    for out, term in zip((p1, p2, p3), terms):
        out[...] = (held_now + term).astype(BF)


def lower_kernel(pos, r1, r2, r3, held, b0, b1, q1, q2, q3, held_out):
    held_now = held[...] + r1[...].astype(F32) + r2[...] + r3[...]
    held_out[...] = held_now
    terms = up_terms(pos[Y], b0[...].astype(F32), b1[...].astype(F32))
    for out, term in zip((q1, q2, q3), terms):
        out[...] = (held_now + term).astype(BF)


def inner_kernel(
    proj, grads, mix, out_t, query_t, key_out, value_out, level_out, table, mixed, score_grad
):
    half = DH
    s_at = lax.broadcasted_iota(jnp.int32, (half, half), 0)
    t_at = lax.broadcasted_iota(jnp.int32, (half, half), 1)
    apart = s_at ^ t_at
    level = jnp.zeros((half, half), jnp.int32)
    for place in range(7):
        level = level + (apart >= (1 << place)).astype(jnp.int32)
    table[...] = jnp.where(s_at <= t_at, level, -1)
    mixed[half:, :half] = jnp.zeros((half, half), BF)
    score_grad[half:, :half] = jnp.zeros((half, half), BF)

    for h, cols in heads():
        qq, kk, vv, gg = proj[0, :, cols], proj[1, :, cols], proj[2, :, cols], grads[:, cols]
        kt = turned(kk).astype(BF)
        vt = turned(vv).astype(BF)
        scores = dot(kk, qq, ((1,), (1,)))
        mix_grad = dot(vv, gg, ((1,), (1,)))

        def row(level, at, h=h):
            return mix[level, h : h + 1, at : at + half] * scale_of(level)

        levels = table[...]
        for at in (0, half):
            score, grad = scores[at : at + half, at : at + half], mix_grad[at : at + half, at : at + half]
            product = score * grad
            weight = jnp.zeros((half, half), F32)
            for level in range(8):
                here = levels == level
                weight = jnp.where(here, row(level, at), weight)
                level_out[level, h : h + 1, at : at + half] = jnp.sum(
                    jnp.where(here, product, 0.0), axis=0, keepdims=True
                ) * scale_of(level)
            mixed[at : at + half, at : at + half] = (weight * score).astype(BF)
            score_grad[at : at + half, at : at + half] = (weight * grad).astype(BF)
        score, grad = scores[:half, half:], mix_grad[:half, half:]
        weight = row(8, half)
        level_out[8, h : h + 1, :half] = jnp.zeros((1, half), F32)
        level_out[8, h : h + 1, half:] = jnp.sum(score * grad, axis=0, keepdims=True) * scale_of(8)
        mixed[:half, half:] = (weight * score).astype(BF)
        score_grad[:half, half:] = (weight * grad).astype(BF)

        out_t[h] = dot(vt, mixed[...], ((1,), (0,)))
        query_t[h] = dot(kt, score_grad[...], ((1,), (0,)))
        key_out[:, cols] = dot(score_grad[...], qq, ((1,), (0,)))
        value_out[:, cols] = dot(mixed[...], gg, ((1,), (0,)))


def key_value_kernel(proj, key_in, value_in, held, ry1, ry2, ry3, grads):
    for _, cols in heads():
        state = held[cols, :] + ry1[cols, :].astype(F32) + ry2[cols, :] + ry3[cols, :]
        state = state.astype(BF)
        grads[0, :, cols] = (key_in[:, cols] + dot(proj[2, :, cols], state, ((1,), (1,)))).astype(
            BF
        )
        grads[1, :, cols] = (
            value_in[:, cols] + dot(proj[1, :, cols], state, ((1,), (0,)))
        ).astype(BF)


def pair_of(p, *parts):
    one, two, three = (a.astype(F32) for a in parts)
    low = one * flag((p == 1) | (p == 3))
    high = one * flag(p == 2) + two * flag(p >= 2) + three * flag(p == 3)
    return low.astype(BF), high.astype(BF)


def query_kernel(pos, out_grad, mix, query_t, *refs):
    parts, (grads, buckets) = refs[:9], refs[9:]
    for h, cols in heads():
        gt = turned(out_grad[:, cols])
        query = query_t[h]
        for line in range(3):
            three = (a[cols, :] for a in parts[3 * line : 3 * line + 3])
            for j, bucket in enumerate(pair_of(pos[(Y, Z, X)[line]], *three), 2 * line):
                buckets[j, cols, :] = bucket
                row = mix[9 + j, h : h + 1, :] * scale_of(9 + j)
                query = query + dot(bucket, (gt * row).astype(BF), ((1,), (0,)))
        grads[0, :, cols] = (query * DH**-0.5).T.astype(BF)


def read_kernel(proj, out_grad, mix, out_t, level_in, buckets, attended, level_out):
    level_out[:9] = level_in[...]
    for h, cols in heads():
        qt = turned(proj[0, :, cols]).astype(BF)
        gt = turned(out_grad[:, cols])
        total = out_t[h]
        for j in range(6):
            row = mix[9 + j, h : h + 1, :] * scale_of(9 + j)
            reads = dot(buckets[j, cols, :], qt, ((0,), (0,)))
            total = total + reads * row
            level_out[9 + j, h : h + 1, :] = jnp.sum(
                reads * gt, axis=0, keepdims=True
            ) * scale_of(9 + j)
        attended[:, cols] = total.T.astype(BF)


def column_kernel(pos, hidden, other, c0, c1, c2, c3, whole):
    core = pos[3]
    outs = (c0, c1, c2, c3)

    @pl.when(core == 0)
    def _():
        whole[:, :1024] = hidden[...]
        whole[:, 1024:] = other[...]
        for step, out in enumerate(outs):
            column = lax.rem(pos[X] + step, 4) * 512
            out[...] = whole[:, pl.ds(pl.multiple_of(column, 512), 512)]

    @pl.when(core == 1)
    def _():
        source = lax.broadcasted_iota(jnp.int32, (512, 128), 0)
        target = lax.broadcasted_iota(jnp.int32, (512, 128), 1)
        start = (target // 32) * 128 + target % 32
        for step, out in enumerate(outs):
            run = lax.rem(pos[Y] + step, 4) * 32
            pick = jnp.where(source == start + run, 1.0, 0.0).astype(BF)
            for tile in range(4):
                half = other if tile < 2 else hidden
                piece = half[:, 512 * (tile % 2) : 512 * (tile % 2) + 512]
                out[:, 128 * tile : 128 * tile + 128] = dot(piece, pick, ((1,), (0,))).astype(BF)


def second_kernel(pos, product, own, o1, o2, o3):
    line = jnp.where(pos[3] == 0, pos[Z], pos[X])
    for step, out in enumerate((own, o1, o2, o3)):
        rows = pl.ds(pl.multiple_of(lax.rem(line + step, 4) * 128, 128), 128)
        out[...] = product[:, rows, :].astype(out.dtype)


def turn_kernel(h0, h1, h2, h3, turned_out):
    for n, block in enumerate((h0, h1, h2, h3)):
        turned_out[:, 256 * n : 256 * n + 256] = turned(block[...]).astype(BF)


def query_second_kernel(pos, columns, g0, g1, g2, g3, own, o1, o2, o3, product):
    total = jnp.zeros((512, 512), F32)
    for n, block in enumerate((g0, g1, g2, g3)):
        total = total + dot(columns[:, 256 * n : 256 * n + 256], block[0], ((1,), (0,)))
    product[0] = total
    second_kernel(pos, product, own, o1, o2, o3)


def third_kernel(
    pos, mine0, mine1, a1, a2, a3, b1, b2, b3, own, o1, o2, o3, total
):
    total[0:1] = mine0[...] + a1[...].astype(F32) + a2[...] + a3[...]
    total[1:3] = mine1[...] + b1[...].astype(F32) + b2[...] + b3[...]
    line = jnp.where(pos[3] == 0, pos[Y], pos[Z])
    for step, out in enumerate((own, o1, o2, o3)):
        rows = pl.ds(pl.multiple_of(lax.rem(line + step, 4) * 32, 32), 32)
        out[...] = total[:, rows, :].astype(out.dtype)


def shape(dims, kind):
    return pltpu.VMEM(dims, kind)


def call(kernel, arrays, outs, pos=None, scratch=()):
    whole = pl.BlockSpec(memory_space=pltpu.VMEM)
    scalars = [] if pos is None else [pl.BlockSpec(memory_space=pltpu.SMEM)]
    run = pl.pallas_call(
        kernel,
        in_specs=scalars + [whole] * len(arrays),
        out_specs=[whole] * len(outs),
        out_shape=outs,
        scratch_shapes=scratch,
        compiler_params=pltpu.CompilerParams(vmem_limit_bytes=8 << 20),
    )
    held = [pltpu.with_memory_space_constraint(a, pltpu.VMEM) for a in arrays]
    return run(*([] if pos is None else [pos]), *held)


def layer(hidden, proj_weights, level_mix, out_grad):
    x, z, y = (lax.axis_index(name) for name in SEQ)
    core = lax.axis_index("head")
    pos = jnp.stack([x, z, y, core]).astype(jnp.int32)
    other = partner(hidden)
    root = jnp.array([DH**-0.5, 1.0, 1.0], F32)[:, None, None]
    near = lax.dynamic_slice_in_dim(proj_weights, 1024 * core, 1024, 0)
    far = lax.dynamic_slice_in_dim(proj_weights, 1024 * (1 - core), 1024, 0)
    near_part = jnp.einsum("td,dme->mte", hidden, near, preferred_element_type=F32)
    far_part = jnp.einsum("td,dme->mte", other, far, preferred_element_type=F32)
    projected = ((near_part + far_part) * root).astype(BF)
    mix = level_mix

    own_columns, *far_columns = call(
        column_kernel,
        [hidden, other],
        [shape((256, 512), BF)] * 4,
        pos,
        [pltpu.VMEM((256, 2048), BF)],
    )
    hidden_blocks = [own_columns]
    for n, block in zip((1, 2, 3), far_columns):
        hidden_blocks.append(shifted(block, (X, Y), n))

    state_shape = shape((512, DH), BF)
    states, b0, b1, b2, b3, b5, u3 = call(
        state_kernel, [projected, out_grad, mix], [state_shape] * 7, pos
    )

    def line_of(axis):
        return (axis, axis)

    def sent(pieces, axis, which="all"):
        out = []
        for n, piece in zip((1, 2, 3), pieces):
            out.append(shifted(piece, line_of(axis), n, which))
        return out

    gy = sent([states] * 3, Y)
    rx = sent([b5, b5, u3], X, "down")
    out_t, query_t, key_in, value_in, level_in = call(
        inner_kernel,
        [projected, out_grad, mix],
        [shape((4, DH, 256), F32)] * 2
        + [shape((256, 512), F32)] * 2
        + [shape((9, 4, 256), F32)],
        scratch=[pltpu.VMEM((DH, DH), jnp.int32)] + [pltpu.VMEM((256, 256), BF)] * 2,
    )
    p1, p2, p3, held = call(
        upper_kernel, [*rx, b2, b3], [state_shape] * 3 + [shape((512, DH), F32)], pos
    )
    uz = sent([p1, p2, p3], Z)
    (group,) = call(gather_kernel, [states, *gy], [state_shape])
    rz = sent([group] * 3, Z)
    q1, q2, q3, held = call(
        lower_kernel, [*uz, held, b0, b1], [state_shape] * 3 + [shape((512, DH), F32)], pos
    )
    ry = sent([q1, q2, q3], Y)
    (group,) = call(gather_kernel, [group, *rz], [state_shape])
    gx = sent([group] * 3, X, "up")
    grads = [None, None]
    (grads[0],) = call(
        key_value_kernel, [projected, key_in, value_in, held, *ry], [shape((2, 256, 512), BF)]
    )
    grads[1], buckets = call(
        query_kernel,
        [out_grad, mix, query_t, *gy, *rz, *gx],
        [shape((1, 256, 512), BF), shape((6, 512, DH), BF)],
        pos,
    )
    attended, level_grad = call(
        read_kernel,
        [projected, out_grad, mix, out_t, level_in, buckets],
        [
            jax.ShapeDtypeStruct((256, 512), BF),
            jax.ShapeDtypeStruct((15, 4, 256), F32),
        ],
    )

    grad_blocks = [[grads[0]], [grads[1]]]
    for i in (0, 1):
        for n in (1, 2, 3):
            grad_blocks[i].append(shifted(grads[i], (X, Y), n))

    all_grads = jnp.concatenate([grads[1], grads[0]], axis=0)
    theirs = jnp.einsum("mte,dme->td", all_grads, far, preferred_element_type=F32)
    mine = lax.optimization_barrier(
        jnp.einsum("mte,dme->td", all_grads, near, preferred_element_type=F32)
    )
    came = partner(theirs)
    input_grad = (mine + came).astype(BF)

    def products(blocks):
        return functools.reduce(
            jnp.add,
            [
                jnp.einsum("td,mte->mde", h, g, preferred_element_type=F32)
                for h, g in zip(hidden_blocks, blocks)
            ],
        )

    key_value_products = products(grad_blocks[0])
    (columns_turned,) = call(turn_kernel, hidden_blocks, [shape((512, 1024), BF)])

    def exchanged(pieces, axes):
        came = []
        for n, piece in zip((1, 2, 3), pieces):
            came.append(shifted(piece, axes, n))
        return came

    def second(product):
        size = product.shape[0]
        own, *pieces = call(
            second_kernel,
            [product],
            [shape((size, 128, 512), F32)] + [shape((size, 128, 512), BF)] * 3,
            pos,
        )
        return own, exchanged(pieces, (Z, X))

    own1, came1 = second(key_value_products)
    own0, *pieces = call(
        query_second_kernel,
        [columns_turned, *grad_blocks[1]],
        [shape((1, 128, 512), F32)] + [shape((1, 128, 512), BF)] * 3,
        pos,
        [pltpu.VMEM((1, 512, 512), F32)],
    )
    came0 = exchanged(pieces, (Z, X))
    own, *pieces = call(
        third_kernel,
        [own0, own1, *came0, *came1],
        [shape((3, 32, 512), F32)] + [shape((3, 32, 512), BF)] * 3,
        pos,
        [pltpu.VMEM((3, 128, 512), F32)],
    )
    came = exchanged(pieces, (Y, Z))
    partial_weights = own + came[0] + came[1] + came[2]
    weight_grad = (partial_weights * 16384**-0.5).transpose(1, 0, 2)
    return (attended, input_grad, weight_grad, level_grad)


def solution(mesh):
    split = Mesh(mesh.devices.reshape(4, 4, 4, 2), ALL)
    return jax.shard_map(
        layer,
        mesh=split,
        in_specs=(P(SEQ, "head"), P(None, None, "head"), P(None, "head", SEQ), P(SEQ, "head")),
        out_specs=(P(SEQ, "head"), P(SEQ, "head"), P(SEQ, None, "head"), P(None, "head", SEQ)),
        check_vma=False,
    )
```

```python
import jax
import jax.numpy as jnp
from jax import lax
from jax.experimental import pallas as pl
from jax.experimental.pallas import tpu as pltpu
from jax.sharding import Mesh
from jax.sharding import PartitionSpec as P


DH = 128
SEQ = ("seq_0", "seq_1", "seq_2")
ALL = SEQ + ("head",)
BF = jnp.bfloat16
F32 = jnp.float32
X, Z, Y = 0, 1, 2


def scale_of(level):
    return 1.0 if level == 0 else 2.0 ** (-(level - 1) / 2)


def places():
    return [
        (x, z, y, h) for x in range(4) for z in range(4) for y in range(4) for h in range(2)
    ]


def index_of(place):
    x, z, y, h = place
    return ((x * 4 + z) * 4 + y) * 2 + h


def shifted(value, axes, step, which="all"):
    pairs = []
    for place in places():
        axis = axes[place[3]]
        target = list(place)
        target[axis] = (place[axis] + step) % 4
        if which == "up" and target[axis] < place[axis]:
            continue
        if which == "down" and target[axis] > place[axis]:
            continue
        pairs.append((index_of(place), index_of(target)))
    return lax.ppermute(value, ALL, pairs)


def partner(value):
    return lax.ppermute(value, "head", [(0, 1), (1, 0)])


def dot(a, b, dims):
    return lax.dot_general(a, b, (dims, ((), ())), preferred_element_type=F32)


def flag(condition):
    return jnp.where(condition, 1.0, 0.0).astype(F32)


def turned(array):
    return array.astype(F32).T


def heads():
    return [(h, slice(h * DH, (h + 1) * DH)) for h in range(4)]


def state_kernel(pos, proj, grads, mix, s_out, b0, b1, b2, b3, b5, u3):
    two = flag(pos[X] == 2)
    for h, cols in heads():
        qt = turned(proj[0, :, cols])
        kt = turned(proj[1, :, cols]).astype(BF)
        gg = grads[:, cols]
        s_out[cols, :] = dot(kt, proj[2, :, cols], ((1,), (0,))).astype(BF)

        def grad(j):
            row = mix[9 + j, h : h + 1, :] * scale_of(9 + j)
            return dot((qt * row).astype(BF), gg, ((1,), (0,)))

        b0[cols, :] = grad(0).astype(BF)
        b1[cols, :] = grad(1).astype(BF)
        b2[cols, :] = grad(2).astype(BF)
        b3[cols, :] = grad(3).astype(BF)
        g4, g5 = grad(4), grad(5)
        b5[cols, :] = g5.astype(BF)
        u3[cols, :] = (g5 * two + g4 * (1.0 - two)).astype(BF)


def up_terms(p, low, high):
    one = high * flag(p == 3)
    two = high * flag(p >= 2)
    three = low * flag((p == 1) | (p == 3)) + high * flag(p == 2)
    return one, two, three


def gather_kernel(mine, a1, a2, a3, group):
    group[...] = (mine[...].astype(F32) + a1[...] + a2[...] + a3[...]).astype(BF)


def upper_kernel(pos, r1, r2, r3, b2, b3, p1, p2, p3, held):
    held_now = r1[...].astype(F32) + r2[...] + r3[...]
    held[...] = held_now
    terms = up_terms(pos[Z], b2[...].astype(F32), b3[...].astype(F32))
    for out, term in zip((p1, p2, p3), terms):
        out[...] = (held_now + term).astype(BF)


def lower_kernel(pos, r1, r2, r3, held, b0, b1, q1, q2, q3, held_out):
    held_now = held[...] + r1[...].astype(F32) + r2[...] + r3[...]
    held_out[...] = held_now
    terms = up_terms(pos[Y], b0[...].astype(F32), b1[...].astype(F32))
    for out, term in zip((q1, q2, q3), terms):
        out[...] = (held_now + term).astype(BF)


def inner_kernel(
    proj, grads, mix, out_t, query_t, key_out, value_out, level_out, table, mixed, score_grad
):
    half = DH
    s_at = lax.broadcasted_iota(jnp.int32, (half, half), 0)
    t_at = lax.broadcasted_iota(jnp.int32, (half, half), 1)
    apart = s_at ^ t_at
    level = jnp.zeros((half, half), jnp.int32)
    for place in range(7):
        level = level + (apart >= (1 << place)).astype(jnp.int32)
    table[...] = jnp.where(s_at <= t_at, level, -1)
    mixed[half:, :half] = jnp.zeros((half, half), BF)
    score_grad[half:, :half] = jnp.zeros((half, half), BF)

    for h, cols in heads():
        qq, kk, vv, gg = proj[0, :, cols], proj[1, :, cols], proj[2, :, cols], grads[:, cols]
        kt = turned(kk).astype(BF)
        vt = turned(vv).astype(BF)
        scores = dot(kk, qq, ((1,), (1,)))
        mix_grad = dot(vv, gg, ((1,), (1,)))

        def row(level, at, h=h):
            return mix[level, h : h + 1, at : at + half] * scale_of(level)

        levels = table[...]
        for at in (0, half):
            score, grad = scores[at : at + half, at : at + half], mix_grad[at : at + half, at : at + half]
            product = score * grad
            weight = jnp.zeros((half, half), F32)
            for level in range(8):
                here = levels == level
                weight = jnp.where(here, row(level, at), weight)
                level_out[level, h : h + 1, at : at + half] = jnp.sum(
                    jnp.where(here, product, 0.0), axis=0, keepdims=True
                ) * scale_of(level)
            mixed[at : at + half, at : at + half] = (weight * score).astype(BF)
            score_grad[at : at + half, at : at + half] = (weight * grad).astype(BF)
        score, grad = scores[:half, half:], mix_grad[:half, half:]
        weight = row(8, half)
        level_out[8, h : h + 1, :half] = jnp.zeros((1, half), F32)
        level_out[8, h : h + 1, half:] = jnp.sum(score * grad, axis=0, keepdims=True) * scale_of(8)
        mixed[:half, half:] = (weight * score).astype(BF)
        score_grad[:half, half:] = (weight * grad).astype(BF)

        out_t[h] = dot(vt, mixed[...], ((1,), (0,)))
        query_t[h] = dot(kt, score_grad[...], ((1,), (0,)))
        key_out[:, cols] = dot(score_grad[...], qq, ((1,), (0,)))
        value_out[:, cols] = dot(mixed[...], gg, ((1,), (0,)))


def key_value_kernel(proj, key_in, value_in, held, ry1, ry2, ry3, grads):
    for _, cols in heads():
        state = held[cols, :] + ry1[cols, :].astype(F32) + ry2[cols, :] + ry3[cols, :]
        state = state.astype(BF)
        grads[0, :, cols] = (key_in[:, cols] + dot(proj[2, :, cols], state, ((1,), (1,)))).astype(
            BF
        )
        grads[1, :, cols] = (
            value_in[:, cols] + dot(proj[1, :, cols], state, ((1,), (0,)))
        ).astype(BF)


def pair_of(p, *parts):
    one, two, three = (a.astype(F32) for a in parts)
    low = one * flag((p == 1) | (p == 3))
    high = one * flag(p == 2) + two * flag(p >= 2) + three * flag(p == 3)
    return low.astype(BF), high.astype(BF)


def query_kernel(pos, out_grad, mix, query_t, *refs):
    parts, (grads, buckets) = refs[:9], refs[9:]
    for h, cols in heads():
        gt = turned(out_grad[:, cols])
        query = query_t[h]
        for line in range(3):
            three = (a[cols, :] for a in parts[3 * line : 3 * line + 3])
            for j, bucket in enumerate(pair_of(pos[(Y, Z, X)[line]], *three), 2 * line):
                buckets[j, cols, :] = bucket
                row = mix[9 + j, h : h + 1, :] * scale_of(9 + j)
                query = query + dot(bucket, (gt * row).astype(BF), ((1,), (0,)))
        grads[0, :, cols] = (query * DH**-0.5).T.astype(BF)


def read_kernel(proj, out_grad, mix, out_t, level_in, buckets, attended, level_out):
    level_out[:9] = level_in[...]
    for h, cols in heads():
        qt = turned(proj[0, :, cols]).astype(BF)
        gt = turned(out_grad[:, cols])
        total = out_t[h]
        for j in range(6):
            row = mix[9 + j, h : h + 1, :] * scale_of(9 + j)
            reads = dot(buckets[j, cols, :], qt, ((0,), (0,)))
            total = total + reads * row
            level_out[9 + j, h : h + 1, :] = jnp.sum(
                reads * gt, axis=0, keepdims=True
            ) * scale_of(9 + j)
        attended[:, cols] = total.T.astype(BF)


def column_kernel(pos, hidden, other, c0, c1, c2, c3, whole):
    core = pos[3]
    outs = (c0, c1, c2, c3)

    @pl.when(core == 0)
    def _():
        whole[:, :1024] = hidden[...]
        whole[:, 1024:] = other[...]
        for step, out in enumerate(outs):
            column = lax.rem(pos[X] + step, 4) * 512
            out[...] = whole[:, pl.ds(pl.multiple_of(column, 512), 512)]

    @pl.when(core == 1)
    def _():
        source = lax.broadcasted_iota(jnp.int32, (512, 128), 0)
        target = lax.broadcasted_iota(jnp.int32, (512, 128), 1)
        start = (target // 32) * 128 + target % 32
        for step, out in enumerate(outs):
            run = lax.rem(pos[Y] + step, 4) * 32
            pick = jnp.where(source == start + run, 1.0, 0.0).astype(BF)
            for tile in range(4):
                half = other if tile < 2 else hidden
                piece = half[:, 512 * (tile % 2) : 512 * (tile % 2) + 512]
                out[:, 128 * tile : 128 * tile + 128] = dot(piece, pick, ((1,), (0,))).astype(BF)


def second_kernel(pos, product, own, o1, o2, o3):
    line = jnp.where(pos[3] == 0, pos[Z], pos[X])
    for step, out in enumerate((own, o1, o2, o3)):
        rows = pl.ds(pl.multiple_of(lax.rem(line + step, 4) * 128, 128), 128)
        out[...] = product[:, rows, :].astype(out.dtype)


def turn_kernel(h0, h1, h2, h3, turned_out):
    for n, block in enumerate((h0, h1, h2, h3)):
        turned_out[:, 256 * n : 256 * n + 256] = turned(block[...]).astype(BF)


def product_kernel(pos, columns, g0, g1, g2, g3, own, o1, o2, o3, product):
    for m in range(product.shape[0]):
        rows = jnp.concatenate([block[m] for block in (g0, g1, g2, g3)], axis=0)
        product[m] = dot(columns[...], rows, ((1,), (0,)))
    second_kernel(pos, product, own, o1, o2, o3)


def third_kernel(
    pos, mine0, mine1, a1, a2, a3, b1, b2, b3, own, o1, o2, o3, total
):
    total[0:1] = mine0[...] + a1[...].astype(F32) + a2[...] + a3[...]
    total[1:3] = mine1[...] + b1[...].astype(F32) + b2[...] + b3[...]
    line = jnp.where(pos[3] == 0, pos[Y], pos[Z])
    for step, out in enumerate((own, o1, o2, o3)):
        rows = pl.ds(pl.multiple_of(lax.rem(line + step, 4) * 32, 32), 32)
        out[...] = total[:, rows, :].astype(out.dtype)


def shape(dims, kind):
    return pltpu.VMEM(dims, kind)


def call(kernel, arrays, outs, pos=None, scratch=()):
    whole = pl.BlockSpec(memory_space=pltpu.VMEM)
    scalars = [] if pos is None else [pl.BlockSpec(memory_space=pltpu.SMEM)]
    run = pl.pallas_call(
        kernel,
        in_specs=scalars + [whole] * len(arrays),
        out_specs=[whole] * len(outs),
        out_shape=outs,
        scratch_shapes=scratch,
        compiler_params=pltpu.CompilerParams(vmem_limit_bytes=12 << 20),
    )
    held = [pltpu.with_memory_space_constraint(a, pltpu.VMEM) for a in arrays]
    return run(*([] if pos is None else [pos]), *held)


def layer(hidden, proj_weights, level_mix, out_grad):
    x, z, y = (lax.axis_index(name) for name in SEQ)
    core = lax.axis_index("head")
    pos = jnp.stack([x, z, y, core]).astype(jnp.int32)
    other = partner(hidden)
    root = jnp.array([DH**-0.5, 1.0, 1.0], F32)[:, None, None]
    near = lax.dynamic_slice_in_dim(proj_weights, 1024 * core, 1024, 0)
    far = lax.dynamic_slice_in_dim(proj_weights, 1024 * (1 - core), 1024, 0)
    near_part = jnp.einsum("td,dme->mte", hidden, near, preferred_element_type=F32)
    far_part = jnp.einsum("td,dme->mte", other, far, preferred_element_type=F32)
    projected = ((near_part + far_part) * root).astype(BF)
    mix = level_mix

    own_columns, *far_columns = call(
        column_kernel,
        [hidden, other],
        [shape((256, 512), BF)] * 4,
        pos,
        [pltpu.VMEM((256, 2048), BF)],
    )
    hidden_blocks = [own_columns]
    for n, block in zip((1, 2, 3), far_columns):
        hidden_blocks.append(shifted(block, (X, Y), n))

    state_shape = shape((512, DH), BF)
    states, b0, b1, b2, b3, b5, u3 = call(
        state_kernel, [projected, out_grad, mix], [state_shape] * 7, pos
    )

    def line_of(axis):
        return (axis, axis)

    def sent(pieces, axis, which="all"):
        out = []
        for n, piece in zip((1, 2, 3), pieces):
            out.append(shifted(piece, line_of(axis), n, which))
        return out

    gy = sent([states] * 3, Y)
    rx = sent([b5, b5, u3], X, "down")
    out_t, query_t, key_in, value_in, level_in = call(
        inner_kernel,
        [projected, out_grad, mix],
        [shape((4, DH, 256), F32)] * 2
        + [shape((256, 512), F32)] * 2
        + [shape((9, 4, 256), F32)],
        scratch=[pltpu.VMEM((DH, DH), jnp.int32)] + [pltpu.VMEM((256, 256), BF)] * 2,
    )
    p1, p2, p3, held = call(
        upper_kernel, [*rx, b2, b3], [state_shape] * 3 + [shape((512, DH), F32)], pos
    )
    uz = sent([p1, p2, p3], Z)
    (group,) = call(gather_kernel, [states, *gy], [state_shape])
    rz = sent([group] * 3, Z)
    q1, q2, q3, held = call(
        lower_kernel, [*uz, held, b0, b1], [state_shape] * 3 + [shape((512, DH), F32)], pos
    )
    ry = sent([q1, q2, q3], Y)
    (group,) = call(gather_kernel, [group, *rz], [state_shape])
    gx = sent([group] * 3, X, "up")
    grads = [None, None]
    (grads[0],) = call(
        key_value_kernel, [projected, key_in, value_in, held, *ry], [shape((2, 256, 512), BF)]
    )
    grads[1], buckets = call(
        query_kernel,
        [out_grad, mix, query_t, *gy, *rz, *gx],
        [shape((1, 256, 512), BF), shape((6, 512, DH), BF)],
        pos,
    )
    attended, level_grad = call(
        read_kernel,
        [projected, out_grad, mix, out_t, level_in, buckets],
        [
            jax.ShapeDtypeStruct((256, 512), BF),
            jax.ShapeDtypeStruct((15, 4, 256), F32),
        ],
    )

    grad_blocks = [[grads[0]], [grads[1]]]
    for i in (0, 1):
        for n in (1, 2, 3):
            grad_blocks[i].append(shifted(grads[i], (X, Y), n))

    all_grads = jnp.concatenate([grads[1], grads[0]], axis=0)
    theirs = jnp.einsum("mte,dme->td", all_grads, far, preferred_element_type=F32)
    mine = lax.optimization_barrier(
        jnp.einsum("mte,dme->td", all_grads, near, preferred_element_type=F32)
    )
    came = partner(theirs)
    input_grad = (mine + came).astype(BF)

    (columns_turned,) = call(turn_kernel, hidden_blocks, [shape((512, 1024), BF)])

    def exchanged(pieces, axes):
        came = []
        for n, piece in zip((1, 2, 3), pieces):
            came.append(shifted(piece, axes, n))
        return came

    def second(blocks):
        size = blocks[0].shape[0]
        own, *pieces = call(
            product_kernel,
            [columns_turned, *blocks],
            [shape((size, 128, 512), F32)] + [shape((size, 128, 512), BF)] * 3,
            pos,
            [pltpu.VMEM((size, 512, 512), F32)],
        )
        return own, exchanged(pieces, (Z, X))

    own1, came1 = second(grad_blocks[0])
    own0, came0 = second(grad_blocks[1])
    own, *pieces = call(
        third_kernel,
        [own0, own1, *came0, *came1],
        [shape((3, 32, 512), F32)] + [shape((3, 32, 512), BF)] * 3,
        pos,
        [pltpu.VMEM((3, 128, 512), F32)],
    )
    came = exchanged(pieces, (Y, Z))
    partial_weights = own + came[0] + came[1] + came[2]
    weight_grad = (partial_weights * 16384**-0.5).transpose(1, 0, 2)
    return (attended, input_grad, weight_grad, level_grad)


def solution(mesh):
    split = Mesh(mesh.devices.reshape(4, 4, 4, 2), ALL)
    return jax.shard_map(
        layer,
        mesh=split,
        in_specs=(P(SEQ, "head"), P(None, None, "head"), P(None, "head", SEQ), P(SEQ, "head")),
        out_specs=(P(SEQ, "head"), P(SEQ, "head"), P(SEQ, None, "head"), P(None, "head", SEQ)),
        check_vma=False,
    )
```
